128 devices in a mesh: slab: 16 (over z, x), pencil: 8 (over y, core).
Axes of the slice: x: 4, y: 4, z: 4, core: 2. Of those that a mesh axis runs over, the one named last changes fastest.
Arguments:
- a_blocks: float32 [256, 64, 20480], P('slab', 'pencil'), may hold values from -1 to 8, as said below
- col_codes: int32 [256, 64, 5], P('slab', 'pencil'), may hold values from 0 to 8, as said below
- agg_of: int32 [256, 64], P('slab', 'pencil'), may hold values from 0 to 2047, as said below
- test_vectors: float32 [256, 64, 2048], P('slab', 'pencil'), may hold values from -36 to 36
Outputs:
- relaxed: float32 [256, 64, 2048], P('slab', 'pencil')
- tiles: float32 [256, 64, 512], P('slab', 'pencil')
- products: float32 [256, 64, 2560], P('slab', 'pencil')
The draws below stay inside these ranges and needn't reach their ends.
Inputs may be any that keep to these rules, and one draw needn't show every extreme that they name: `col_codes`: slot 0 of every block row is code 4, the block row itself; slots 1 to 4 hold different codes among the other eight of the 3 x 3 neighbourhood. `agg_of`: aggregate g is owned by device g // 16, devices numbered slab-major. On each device the block rows, in row-major order, form 64 groups of 2 consecutive block rows; all block rows of a group belong to aggregates of one owner, and the groups of one device go to different owners. Some owners receive a group from every device. `a_blocks`: the diagonal entries of every slot-0 block lie in [1.99, 8].
All inputs are finite; a program needn't handle non-finite values.
Results may differ from the reference program's by a relative error of at most 0.0003.
Values sent between devices are 32-bit elements; how exact they have to be, the bound alone decides.
A program may use at most 320 MiB of HBM per device.

```python
import math
import jax
import jax.numpy as jnp
from jax import lax

BLK = 64
NV = 32
NC = 8
KS = 5
ITERS = 2
BS_DEV = 16
BP_DEV = 8
NBS = 256
NBP = 64
CAP = 2
GROUPS = 64
HOT = 8
AGG_DEV = 16
NAGG = 2048


def draw_a_blocks(key, part):
    off_key, diag_key = jax.random.split(jax.random.fold_in(key, 7))
    offdiag = 0.05 * jax.random.normal(off_key, (NBS, NBP, KS, BLK, BLK), jnp.float32)
    diagonal = jnp.exp(jax.random.uniform(diag_key, (NBS, NBP, BLK), jnp.float32, 0.6931, 2.0794))
    identity = jnp.eye(BLK, dtype=jnp.float32)
    self_block = offdiag[:, :, 0] * (1.0 - identity) + diagonal[:, :, :, None] * identity
    whole = jnp.concatenate([self_block[:, :, None], offdiag[:, :, 1:]], axis=2)
    return whole.reshape(NBS, NBP, KS * BLK * BLK).astype(jnp.float32)


def draw_col_codes(key, part):
    scores = jax.random.randint(jax.random.fold_in(key, 5), (NBS, NBP, 8), 0, 1024) * 16 + jnp.arange(8, dtype=jnp.int32)
    ranked = jnp.argsort(-scores, axis=-1)[:, :, :KS - 1].astype(jnp.int32)
    others = jnp.where(ranked < 4, ranked, ranked + 1)
    centre = jnp.full((NBS, NBP, 1), 4, jnp.int32)
    return jnp.concatenate([centre, others], axis=-1).astype(jnp.int32)


def draw_agg_of(key, part):
    n_slab = NBS // BS_DEV
    n_pencil = NBP // BP_DEV
    devices = n_slab * n_pencil
    rows_dev = BS_DEV * BP_DEV
    hot_key, dev_key = jax.random.split(jax.random.fold_in(key, 11))
    hot_scores = jax.random.randint(hot_key, (devices,), 0, 4096) * devices + jnp.arange(devices, dtype=jnp.int32)
    hot_rank = jnp.argsort(jnp.argsort(-hot_scores))
    is_hot = (hot_rank < HOT).astype(jnp.int32)

    def one_device(dev_seed):
        score_key, order_key, local_key = jax.random.split(dev_seed, 3)
        scores = jax.random.randint(score_key, (devices,), 0, 4096) * devices + jnp.arange(devices, dtype=jnp.int32) + is_hot * (4096 * devices)
        chosen = jnp.argsort(-scores)[:GROUPS].astype(jnp.int32)
        owners = chosen[jax.random.permutation(order_key, GROUPS)]
        local = jax.random.randint(local_key, (GROUPS, CAP), 0, AGG_DEV)
        return (owners[:, None] * AGG_DEV + local).reshape(rows_dev)
    device_share = jax.vmap(one_device)(jax.random.split(dev_key, devices))
    grid = device_share.reshape(n_slab, n_pencil, BS_DEV, BP_DEV)
    return grid.transpose(0, 2, 1, 3).reshape(NBS, NBP).astype(jnp.int32)


def draw_test_vectors(key, part):
    base_key = jax.random.fold_in(jax.random.fold_in(key, 3), 0)
    rising = 1.0 + 2.0 * jnp.arange(NBS, dtype=jnp.float32) / max(NBS - 1, 1)
    values = jnp.clip(jax.random.normal(base_key, (NBS, NBP, BLK * NV), jnp.float32), -6.0, 6.0)
    return (values * rising[:, None, None]).astype(jnp.float32)


def setup_inputs(seed: int = 0) -> dict:
    arg_keys = jax.random.split(jax.random.key(seed), 5)
    a_blocks = draw_a_blocks(jax.random.fold_in(arg_keys[4], 71), 0)
    col_codes = draw_col_codes(jax.random.fold_in(arg_keys[4], 71), 0)
    agg_of = draw_agg_of(jax.random.fold_in(arg_keys[4], 71), 0)
    test_vectors = draw_test_vectors(jax.random.fold_in(arg_keys[4], 71), 0)
    return {"a_blocks": a_blocks, "col_codes": col_codes, "agg_of": agg_of, "test_vectors": test_vectors}


OMEGA = 2.0 / 3.0
FULL_PRECISION = lax.Precision.HIGHEST

def coarse_modes(cells, coarse):
    centre = jnp.arange(cells, dtype=jnp.float32) + 0.5
    order = jnp.arange(coarse, dtype=jnp.float32)
    return jnp.cos(math.pi * centre[:, None] * order[None, :] / cells)

def solve_maps(coarse):
    gram = jnp.einsum('gkv,glv->gkl', coarse, coarse, precision=FULL_PRECISION)
    trace_sum = jnp.trace(gram, axis1=1, axis2=2)
    ridge = 0.1 * trace_sum / NC + 1e-06
    gram = gram + ridge[:, None, None] * jnp.eye(NC, dtype=jnp.float32)[None]
    lower = jnp.linalg.cholesky(gram)
    half_solved = jax.scipy.linalg.solve_triangular(lower, coarse, lower=True)
    solved = jax.scipy.linalg.solve_triangular(lower, half_solved, lower=True, trans=1)
    return jnp.swapaxes(solved, 1, 2)

def apply_rows(blocks, field, col_codes, form):
    padded = jnp.pad(field, ((1, 1), (1, 1), (0, 0), (0, 0)))
    across_index = jnp.arange(NBP, dtype=jnp.int32)

    def one_row(row_index):
        window = lax.dynamic_slice_in_dim(padded, row_index, 3, 0)
        codes = lax.dynamic_index_in_dim(col_codes, row_index, 0, keepdims=False)
        row_blocks = lax.dynamic_index_in_dim(blocks, row_index, 0, keepdims=False)
        picked = window[codes // 3, across_index[:, None] + codes % 3]
        return jnp.einsum(form, row_blocks, picked, precision=FULL_PRECISION)
    return lax.map(one_row, jnp.arange(NBS, dtype=jnp.int32))

def reference(a_blocks, col_codes, agg_of, test_vectors):
    blocks = a_blocks.reshape(NBS, NBP, KS, BLK, BLK)
    diagonal = jnp.diagonal(blocks[:, :, 0], axis1=-2, axis2=-1)
    candidate_vectors = test_vectors.reshape(NBS, NBP, BLK, NV)
    for sweep in range(ITERS):
        image = apply_rows(blocks, candidate_vectors, col_codes, 'jkoc,jkcw->jow')
        candidate_vectors = candidate_vectors - OMEGA * image / diagonal[:, :, :, None]
    squares = lax.optimization_barrier(jnp.sum(candidate_vectors * candidate_vectors, axis=(0, 1, 2)))
    scale = jnp.sqrt(squares / (NBS * NBP * BLK) + 1e-06)
    relaxed = candidate_vectors / scale
    near_null_modes = coarse_modes(BLK, NC)
    flat_rows = relaxed.reshape(NBS * NBP, BLK, NV)
    coef = jnp.einsum('ck,rcv->rkv', near_null_modes, flat_rows, precision=FULL_PRECISION)
    agg_ids = agg_of.reshape(-1)
    counts = jax.ops.segment_sum(jnp.ones(agg_ids.shape, jnp.float32), agg_ids, num_segments=NAGG)
    summed = jax.ops.segment_sum(coef, agg_ids, num_segments=NAGG)
    coarse = summed / jnp.maximum(counts, 1.0)[:, None, None]
    maps = solve_maps(coarse)
    tile_rows = jnp.einsum('rcv,rvk->rck', flat_rows, maps[agg_ids], precision=FULL_PRECISION)
    tile_grid = tile_rows.reshape(NBS, NBP, BLK, NC)
    products = apply_rows(blocks, tile_grid, col_codes, 'jkoc,jkcw->jkow')
    return (relaxed.reshape(NBS, NBP, BLK * NV), tile_grid.reshape(NBS, NBP, BLK * NC), products.reshape(NBS, NBP, KS * BLK * NC))
```

```python
import math

import numpy as np
import jax
import jax.numpy as jnp
from jax import lax
from jax.experimental import pallas as pl
from jax.experimental.pallas import tpu as pltpu
from jax.sharding import PartitionSpec as P

BLK = 64
NV = 32
NC = 8
KS = 5
OMEGA = 2.0 / 3.0
MESH = pl.DeviceIdType.MESH
F32 = jnp.float32
BF16 = jnp.bfloat16

H = 16
W = 8
PW = W + 2
NB = 4

DIRS = [(1, 0), (-1, 0), (0, 1), (0, -1), (1, 1), (1, -1), (-1, 1), (-1, -1)]


def lanes(shape):
    return lax.broadcasted_iota(jnp.int32, shape, len(shape) - 1)


def lane_group(shape):
    return lanes(shape) // NV


def split2(x):
    hi = x.astype(BF16).astype(F32)
    return hi, x - hi


def split3(x):
    one = x.astype(BF16)
    rest = x - one.astype(F32)
    two = rest.astype(BF16)
    three = (rest - two.astype(F32)).astype(BF16)
    return one, two, three


def by_group(parts, group):
    out = parts[3]
    for n in (2, 1, 0):
        out = jnp.where(group == n, parts[n], out)
    return out


def body(n_slab, n_pencil, a_hbm, codes, agg_s, agg_v, tv, qpat, out_v, out_t, out_p,
         abuf, aprep, dinv, vf, pan0, pan1, tp, vc, tmp, colsend, hrow, hcol, hcor,
         pay, send1, recv1, send2, recv2, xg, xrow, xcol, xcor,
         a_sem, hs_sem, hr_sem, s1, r1, s2, r2):
    devices = n_slab * n_pencil
    slab = lax.axis_index("slab")
    pencil = lax.axis_index("pencil")
    me = slab * n_pencil + pencil

    def a_copy(i):
        return pltpu.make_async_copy(
            a_hbm.at[i], abuf.at[lax.rem(i, NB)], a_sem.at[lax.rem(i, NB)]
        )

    for i in range(NB):
        a_copy(i).start()

    barrier = pltpu.get_barrier_semaphore()

    @pl.loop(1, devices)
    def _(n):
        d = lax.rem(me + n, devices)
        pl.semaphore_signal(
            barrier, inc=1, device_id=(d // n_pencil, lax.rem(d, n_pencil)), device_id_type=MESH
        )

    group16 = lane_group((16, 128))
    group64 = lane_group((64, 128))
    odd64 = lax.rem(group64, 2) == 1

    def spread(x, dst, *lead):
        turns = [x] + [pltpu.roll(x, NV * n, 1) for n in (1, 2, 3)]
        for s in range(4):
            dst[(*lead, pl.ds(s, 16, stride=4), slice(None))] = by_group(
                [turns[(g - s) % 4] for g in range(4)], group16
            )

    def panel_of(v):
        hi, lo = split2(v)
        return jnp.where(odd64, lo, hi).astype(BF16)

    def gather_cells(b):
        return by_group([vf[b, pl.ds(s, 16, stride=4), :] for s in range(4)], group16)

    def edge_copies(rnd, rows):
        copies = []
        for n, (ds, dp) in enumerate(DIRS):
            if dp == 0:
                edge = (H - 1) if ds == 1 else 0
                src = rows.at[edge]
                dst = hrow.at[rnd, n]
            elif ds == 0:
                src = colsend.at[rnd, n - 2]
                dst = hcol.at[rnd, n - 2]
            else:
                edge = (H - 1) if ds == 1 else 0
                src = colsend.at[rnd, 0 if dp == 1 else 1, pl.ds(edge * 16, 16)]
                dst = hcor.at[rnd, n - 4]
            copies.append(remote(src, dst, rnd, n))
        return copies

    def remote(src, dst, rnd, n):
        ds, dp = DIRS[n]
        return pltpu.make_async_remote_copy(
            src_ref=src,
            dst_ref=dst,
            send_sem=hs_sem.at[rnd, n],
            recv_sem=hr_sem.at[rnd, n],
            device_id=(lax.rem(slab + ds + n_slab, n_slab), lax.rem(pencil + dp + n_pencil, n_pencil)),
            device_id_type=MESH,
        )

    def from_inside(n):
        ds, dp = DIRS[n]
        ok_s = slab - ds
        ok_p = pencil - dp
        return jnp.logical_and(
            jnp.logical_and(ok_s >= 0, ok_s < n_slab), jnp.logical_and(ok_p >= 0, ok_p < n_pencil)
        )

    def take_edges(rnd, pan):
        for n, (ds, dp) in enumerate(DIRS):
            keep = from_inside(n).astype(F32)
            if dp == 0:
                base = 0 if ds == 1 else (H + 1) * PW
                for j in range(W):
                    spread(hrow[rnd, n, pl.ds(j, 16, stride=8), :] * keep, tmp, j)
                    pan[base + j + 1] = panel_of(tmp[j])
            elif ds == 0:
                col = 0 if dp == 1 else W + 1

                @pl.loop(0, H // 4)
                def _(q):
                    for u in range(4):
                        i = q * 4 + u
                        start = pl.multiple_of(i * 16, 16)
                        spread(hcol[rnd, n - 2, pl.ds(start, 16), :] * keep, tmp, u)
                        pan[(i + 1) * PW + col] = panel_of(tmp[u])
            else:
                spot = (0 if ds == 1 else H + 1) * PW + (0 if dp == 1 else W + 1)
                spread(hcor[rnd, n - 4] * keep, tmp, n)
                pan[spot] = panel_of(tmp[n])

    for i in range(H):
        colsend[0, 0, i * 16:(i + 1) * 16, :] = tv[i, pl.ds(W - 1, 16, stride=8), :]
        colsend[0, 1, i * 16:(i + 1) * 16, :] = tv[i, pl.ds(0, 16, stride=8), :]
    pl.semaphore_wait(barrier, devices - 1)
    edges0 = edge_copies(0, tv)
    for c in edges0:
        c.start()

    lane32 = lanes((32, 128))
    row32 = lax.broadcasted_iota(jnp.int32, (32, 128), 0)
    left = lane32 < 64

    def eight_rows(even, odd):
        parts = []
        for r in range(4):
            parts += [even[r * 8:(r + 1) * 8], odd[r * 8:(r + 1) * 8]]
        return jnp.concatenate(parts, axis=0)

    @pl.loop(0, H)
    def _(i):
        for j in range(W):
            b = i * W + j
            spread(tv[i, pl.ds(j, 16, stride=8), :], vf, b)
            pan0[(i + 1) * PW + j + 1] = panel_of(vf[b])
        a_copy(i).wait()
        slot = lax.rem(i, NB)
        for j in range(W):
            b = i * W + j
            for k in range(KS):
                x = abuf[slot, pl.ds(k * 256 + j, 32, stride=8), :]
                hi, lo = split2(x)
                even = jnp.where(left, hi, pltpu.roll(lo, 64, 1))
                odd = jnp.where(left, pltpu.roll(hi, 64, 1), lo)
                aprep[b * KS + k] = eight_rows(even, odd).astype(BF16)
                if k == 0:
                    d_even = jnp.sum(jnp.where(lane32 == 2 * row32, x, 0.0), axis=1, keepdims=True)
                    d_odd = jnp.sum(jnp.where(lane32 == 2 * row32 + 65, x, 0.0), axis=1, keepdims=True)
                    dinv[b] = jnp.broadcast_to(OMEGA / eight_rows(d_even, d_odd), (64, 128))

        @pl.when(i + NB < H)
        def _():
            a_copy(i + NB).start()

    for c in edges0:
        c.wait_recv()
    take_edges(0, pan0)

    def slot_spots(i, j):
        b = i * W + j
        spots = []
        for k in range(KS):
            code = codes[b * KS + k]
            di = (code * 11) >> 5
            spots.append((i + di) * PW + j + code - 3 * di)
        return spots

    def relax(i, j, old, new):
        b = i * W + j
        left_side = jnp.concatenate([aprep[b * KS + k] for k in range(KS)], axis=1)
        right = []
        for spot in slot_spots(i, j):
            p = old[spot]
            right += [p, p]
        image = jnp.dot(left_side, jnp.concatenate(right, axis=0), preferred_element_type=F32)
        image = image + pltpu.roll(image, NV, 1)
        step = image * dinv[b]
        for r in range(4):
            for p in range(2):
                tmp[j, pl.ds(r * 16 + p, 8, stride=2), :] = step[(2 * r + p) * 8:(2 * r + p + 1) * 8]
        v = vf[b] - tmp[j]
        vf[b] = v
        new[(i + 1) * PW + j + 1] = panel_of(v)

    def keep_cells(i, j, rnd):
        x = gather_cells(i * W + j)
        vc[i, pl.ds(j, 16, stride=8), :] = x
        if j in (0, W - 1):
            colsend[rnd, 0 if j else 1, pl.ds(pl.multiple_of(i * 16, 16), 16), :] = x

    @pl.loop(0, 2)
    def _(n):
        for j in range(W):
            relax(n * (H - 1), j, pan0, pan1)
        for j in range(W):
            keep_cells(n * (H - 1), j, 1)

    @pl.loop(1, H - 1)
    def _(i):
        for j in (0, W - 1):
            relax(i, j, pan0, pan1)
        for j in (0, W - 1):
            keep_cells(i, j, 1)

    edges1 = edge_copies(1, vc)
    for c in edges1:
        c.start()

    @pl.loop(1, H - 1)
    def _(i):
        for j in range(1, W - 1):
            relax(i, j, pan0, pan1)

    for c in edges1:
        c.wait()
    take_edges(1, pan1)

    @pl.loop(0, H)
    def _(i):
        for j in range(W):
            relax(i, j, pan1, pan0)
        for j in range(W):
            keep_cells(i, j, 2)

    edges2 = edge_copies(2, vc)
    for c in edges2:
        c.start()

    group8 = lane_group((8, 128))

    def coefficients(i, squares):
        sums = [None] * NC
        for q in range(16):
            x = vc[i, q * 8:(q + 1) * 8, :]
            squares = squares + x * x
            for m in range(NC):
                term = x * qpat[m * 16 + q:m * 16 + q + 1, :]
                sums[m] = term if sums[m] is None else sums[m] + term
        folded = []
        for m in range(NC):
            y = sums[m] + pltpu.roll(sums[m], 64, 1)
            folded.append(y + pltpu.roll(y, 32, 1))
        start = pl.multiple_of(i * 8, 8)
        pay[pl.ds(start, 8), 0:128] = by_group(folded[:4], group8)
        pay[pl.ds(start, 8), 128:256] = by_group(folded[4:], group8)
        return squares

    squares = lax.fori_loop(0, H, coefficients, jnp.zeros((8, 128), F32))
    squares = jnp.sum(squares, axis=0, keepdims=True)
    squares = squares + pltpu.roll(squares, 64, 1)
    squares = squares + pltpu.roll(squares, 32, 1)

    lane_d = lanes((devices, 128))
    row_d = lax.broadcasted_iota(jnp.int32, (devices, 128), 0)
    agg = agg_v[...]
    mine = jnp.broadcast_to(agg >> 4, (devices, 128)) == row_d
    local = jnp.broadcast_to((agg & 15) + 1, (devices, 128)).astype(F32)
    parity = lane_d & 1
    parts = jnp.concatenate(split3(pay[...]), axis=0)
    group_d = lane_d // NV
    fifth = jnp.broadcast_to(squares, (devices, 128))
    for cap in range(2):
        chosen = jnp.logical_and(mine, parity == cap).astype(F32)
        chosen_b = chosen.astype(BF16)
        packed = jnp.dot(
            jnp.concatenate([chosen_b] * 3, axis=1), parts, preferred_element_type=F32
        )
        send1[pl.ds(2 * cap, devices, stride=8), :] = packed[:, 0:128]
        send1[pl.ds(2 * cap + 1, devices, stride=8), :] = packed[:, 128:256]
        ident = jnp.sum(chosen * local, axis=1, keepdims=True)
        fifth = jnp.where(group_d == cap + 1, ident, fifth)
    send1[pl.ds(4, devices, stride=8), :] = fifth

    my_rows = pl.ds(pl.multiple_of(me * 8, 8), 8)

    @pl.loop(1, devices)
    def _(n):
        d = lax.rem(me + n, devices)
        pltpu.make_async_remote_copy(
            src_ref=send1.at[pl.ds(pl.multiple_of(d * 8, 8), 8)],
            dst_ref=recv1.at[my_rows],
            send_sem=s1,
            recv_sem=r1,
            device_id=(d // n_pencil, lax.rem(d, n_pencil)),
            device_id_type=MESH,
        ).start()

    own = pltpu.make_async_copy(send1.at[my_rows], recv1.at[my_rows], r1)
    own.start()
    for c in edges2:
        c.wait()
    take_edges(2, pan0)
    pltpu.make_async_copy(send1, recv1, r1).wait()

    heard = recv1[pl.ds(4, devices, stride=8), :]
    total = jnp.sum(heard, axis=0, keepdims=True)
    lane1 = lanes((1, 128))
    total = jnp.where(lane1 < NV, total, 0.0)
    total = total + pltpu.roll(total, 64, 1)
    total = total + pltpu.roll(total, 32, 1)
    inv = 1.0 / jnp.sqrt(total / (H * W * BLK * devices) + 1e-06)

    want = (lane_d + 1).astype(F32)
    few = lane_d < 16
    member_t = [
        jnp.where(jnp.logical_and(pltpu.roll(heard, 128 - NV * (cap + 1), 1) == want, few), 1.0, 0.0)
        for cap in range(2)
    ]
    member = [m.T[0:16] for m in member_t]
    counts = jnp.sum(member[0] + member[1], axis=1, keepdims=True)
    lhs, rhs = [], []
    for cap in range(2):
        rows = jnp.concatenate(
            [recv1[pl.ds(2 * cap + h, devices, stride=8), :] for h in range(2)], axis=1
        )
        lhs += [member[cap].astype(BF16)] * 3
        rhs += list(split3(rows))
    coarse = jnp.dot(
        jnp.concatenate(lhs, axis=1), jnp.concatenate(rhs, axis=0), preferred_element_type=F32
    )
    coarse = coarse * jnp.concatenate([inv, inv], axis=1) / jnp.maximum(counts, 1.0)
    in_first = lanes((16, 128)) < NV
    fit = []
    for k in range(NC):
        half = coarse[:, 128 * (k // 4):128 * (k // 4) + 128]
        if k % 4:
            half = pltpu.roll(half, 128 - NV * (k % 4), 1)
        fit.append(jnp.where(in_first, half, 0.0))
    gram = {}
    for k in range(NC):
        for l in range(k + 1):
            gram[k, l] = jnp.sum(fit[k] * fit[l], axis=1, keepdims=True)
    trace_sum = gram[0, 0]
    for k in range(1, NC):
        trace_sum = trace_sum + gram[k, k]
    ridge = 0.1 * trace_sum / NC + 1e-06
    low, raw, pivot = {}, {}, {}
    for k in range(NC):
        top = gram[k, k] + ridge
        for l in range(k):
            top = top - raw[k, l] * low[k, l]
        pivot[k] = 1.0 / top
        for m in range(k + 1, NC):
            val = gram[m, k]
            for l in range(k):
                val = val - raw[m, l] * low[k, l]
            raw[m, k] = val
            low[m, k] = val * pivot[k]
    sol = []
    for k in range(NC):
        y = fit[k]
        for l in range(k):
            y = y - low[k, l] * sol[l]
        sol.append(y)
    for k in range(NC):
        sol[k] = sol[k] * pivot[k]
    for k in reversed(range(NC)):
        for l in range(k + 1, NC):
            sol[k] = sol[k] - low[l, k] * sol[l]
    columns = []
    for k in range(NC):
        x = sol[k] * inv
        first = x + pltpu.roll(x, 64, 1)
        columns.append(jnp.concatenate([first, pltpu.roll(first, 32, 1)], axis=0))
    table = jnp.concatenate(columns, axis=1)
    pieces = [p for p in split3(table)]
    table = jnp.concatenate(pieces + [jnp.zeros_like(pieces[0])], axis=0)
    pick = member_t[0] + pltpu.roll(member_t[1], 16, 1)
    pick = pick + pltpu.roll(pick, 32, 1) + pltpu.roll(pick, 64, 1)
    replies = jnp.dot(pick.astype(BF16), table, preferred_element_type=F32)
    for k in range(NC):
        send2[pl.ds(k, devices, stride=8), :] = replies[:, 128 * k:128 * (k + 1)]

    @pl.loop(1, devices)
    def _(n):
        d = lax.rem(me + n, devices)
        pltpu.make_async_remote_copy(
            src_ref=send2.at[pl.ds(pl.multiple_of(d * 8, 8), 8)],
            dst_ref=recv2.at[me],
            send_sem=s2,
            recv_sem=r2,
            device_id=(d // n_pencil, lax.rem(d, n_pencil)),
            device_id_type=MESH,
        ).start()

    own = pltpu.make_async_copy(send2.at[my_rows], recv2.at[me], r2)
    own.start()

    @pl.loop(0, H)
    def _(i):
        out_v[i] = vc[i] * inv

    pltpu.make_async_copy(recv2, recv2, r2).wait()

    @pl.loop(0, H)
    def _(i):
        for g in range(W // 2):
            xg[i, g] = recv2[agg_s[i * W + 2 * g] >> 4]

    edges3 = []
    for n, (ds, dp) in enumerate(DIRS):
        if dp == 0:
            edge = (H - 1) if ds == 1 else 0
            edges3.append(remote(xg.at[edge], xrow.at[n], 3, n))
        elif ds == 0:
            edges3.append(remote(xg.at[:, (W // 2 - 1) if dp == 1 else 0], xcol.at[n - 2], 3, n))
        else:
            edge = (H - 1) if ds == 1 else 0
            edges3.append(
                remote(xg.at[edge, (W // 2 - 1) if dp == 1 else 0], xcor.at[n - 4], 3, n)
            )
    for c in edges3:
        c.start()

    even8 = lax.rem(group8, 2) == 0
    high8 = group8 < 2

    def make_tile(spot, x, cap):
        x = jnp.where(even8 if cap == 0 else jnp.logical_not(even8), x, pltpu.roll(x, NV, 1))
        hi, lo = split2(x)
        w = jnp.where(high8, hi, lo)
        w = jnp.concatenate([w] * 16, axis=0).astype(BF16)
        t = lax.dot_general(
            pan0[spot], w, (((1,), (1,)), ((), ())), preferred_element_type=F32
        )
        hi, lo = split2(t)
        tp[spot] = jnp.concatenate([hi, lo], axis=1).astype(BF16)
        return t

    lane8 = lanes((8, 128)) // NC
    sub8 = lax.broadcasted_iota(jnp.int32, (8, 128), 0)
    sub4 = lax.broadcasted_iota(jnp.int32, (4, 128), 0)

    def four_rows(vregs):
        rows = [jnp.sum(v, axis=0, keepdims=True) for v in vregs]
        return jnp.concatenate(rows, axis=0)

    @pl.loop(0, H)
    def _(i):
        for j in range(W):
            t = make_tile((i + 1) * PW + j + 1, xg[i, j // 2], j % 2)
            vregs = [
                jnp.where(
                    lane8 == sub8,
                    t[r * 16:r * 16 + 8],
                    jnp.where(lane8 == sub8 + 8, t[r * 16 + 8:r * 16 + 16], 0.0),
                )
                for r in range(4)
            ]
            out_t[i, pl.ds(j, 4, stride=8), :] = four_rows(vregs)

    for c in edges3:
        c.wait()
    for n, (ds, dp) in enumerate(DIRS):
        if dp == 0:
            base = 0 if ds == 1 else (H + 1) * PW
            for j in range(W):
                make_tile(base + j + 1, xrow[n, j // 2], j % 2)
        elif ds == 0:
            col = 0 if dp == 1 else W + 1

            @pl.loop(0, H // 4)
            def _(q):
                for u in range(4):
                    i = q * 4 + u
                    make_tile((i + 1) * PW + col, xcol[n - 2, i], 1 if dp == 1 else 0)
        else:
            spot = (0 if ds == 1 else H + 1) * PW + (0 if dp == 1 else W + 1)
            make_tile(spot, xcor[n - 4], 1 if dp == 1 else 0)

    @pl.loop(0, H)
    def _(i):
        for j in range(W):
            spots = slot_spots(i, j)
            for k in range(KS):
                t = tp[spots[k]]
                o = jnp.dot(
                    aprep[(i * W + j) * KS + k],
                    jnp.concatenate([t, t], axis=0),
                    preferred_element_type=F32,
                )
                o = o[:, 0:128] + o[:, 128:256]
                vregs = [
                    jnp.where(
                        lane8 == 2 * sub8,
                        o[r * 16:r * 16 + 8],
                        jnp.where(lane8 == 2 * sub8 + 1, o[r * 16 + 8:r * 16 + 16], 0.0),
                    )
                    for r in range(4)
                ]
                out_p[i, pl.ds(k * 32 + j, 4, stride=8), :] = four_rows(vregs)

    for c in edges0:
        c.wait_send()
    others = pl.ds(0, (devices - 1) * 8)
    pltpu.make_async_copy(send1.at[others], recv1.at[others], s1).wait()
    pltpu.make_async_copy(send2.at[others], send2.at[others], s2).wait()


def mode_rows():
    centre = np.arange(BLK, dtype=np.float64) + 0.5
    table = np.cos(math.pi * centre[:, None] * np.arange(NC)[None, :] / BLK)
    rows = table.reshape(16, 4, NC).transpose(2, 0, 1).reshape(NC * 16, 4)
    return np.repeat(rows, NV, axis=1).astype(np.float32)


def solution(mesh):
    n_slab = mesh.shape["slab"]
    n_pencil = mesh.shape["pencil"]
    devices = n_slab * n_pencil

    def shards(a_blocks, col_codes, agg_of, test_vectors):
        a = a_blocks.reshape(H, W, 160, 128).transpose(0, 2, 1, 3).reshape(H, 1280, 128)
        tv = test_vectors.reshape(H, W, 16, 128).transpose(0, 2, 1, 3).reshape(H, 128, 128)
        codes = col_codes.reshape(H * W * KS)
        agg = agg_of.reshape(H * W)
        vmem = pl.BlockSpec(memory_space=pltpu.VMEM)
        smem = pl.BlockSpec(memory_space=pltpu.SMEM)
        out_v, out_t, out_p = pl.pallas_call(
            lambda *refs: body(n_slab, n_pencil, *refs),
            out_shape=(
                jax.ShapeDtypeStruct((H, 128, 128), F32),
                jax.ShapeDtypeStruct((H, 32, 128), F32),
                jax.ShapeDtypeStruct((H, 160, 128), F32),
            ),
            in_specs=[pl.BlockSpec(memory_space=pl.ANY), smem, smem, vmem, vmem, vmem],
            out_specs=(vmem, vmem, vmem),
            scratch_shapes=[
                pltpu.VMEM((NB, 1280, 128), F32),
                pltpu.VMEM((H * W * KS, 64, 128), BF16),
                pltpu.VMEM((H * W, 64, 128), F32),
                pltpu.VMEM((H * W, 64, 128), F32),
                pltpu.VMEM(((H + 2) * PW, 64, 128), BF16),
                pltpu.VMEM(((H + 2) * PW, 64, 128), BF16),
                pltpu.VMEM(((H + 2) * PW, 64, 256), BF16),
                pltpu.VMEM((H, 128, 128), F32),
                pltpu.VMEM((8, 64, 128), F32),
                pltpu.VMEM((3, 2, 256, 128), F32),
                pltpu.VMEM((3, 2, 128, 128), F32),
                pltpu.VMEM((3, 2, 256, 128), F32),
                pltpu.VMEM((3, 4, 16, 128), F32),
                pltpu.VMEM((128, 256), F32),
                pltpu.VMEM((devices * 8, 128), F32),
                pltpu.VMEM((devices * 8, 128), F32),
                pltpu.VMEM((devices * 8, 128), F32),
                pltpu.VMEM((devices, 8, 128), F32),
                pltpu.VMEM((H, W // 2, 8, 128), F32),
                pltpu.VMEM((2, W // 2, 8, 128), F32),
                pltpu.VMEM((2, H, 8, 128), F32),
                pltpu.VMEM((4, 8, 128), F32),
                pltpu.SemaphoreType.DMA((NB,)),
                pltpu.SemaphoreType.DMA((4, 8)),
                pltpu.SemaphoreType.DMA((4, 8)),
                pltpu.SemaphoreType.DMA,
                pltpu.SemaphoreType.DMA,
                pltpu.SemaphoreType.DMA,
                pltpu.SemaphoreType.DMA,
            ],
            compiler_params=pltpu.CompilerParams(
                collective_id=0, has_side_effects=True, vmem_limit_bytes=60 * 1024 * 1024
            ),
        )(a, codes, agg, agg.reshape(1, 128), tv, jnp.asarray(mode_rows()))
        relaxed = out_v.reshape(H, 16, W, 128).transpose(0, 2, 1, 3).reshape(H, W, BLK * NV)
        tiles = out_t.reshape(H, 4, W, 128).transpose(0, 2, 1, 3).reshape(H, W, BLK * NC)
        products = out_p.reshape(H, 20, W, 128).transpose(0, 2, 1, 3).reshape(H, W, KS * BLK * NC)
        return relaxed, tiles, products

    spec = P("slab", "pencil", None)
    return jax.shard_map(
        shards,
        mesh=mesh,
        in_specs=(spec, spec, P("slab", "pencil"), spec),
        out_specs=(spec, spec, spec),
        check_vma=False,
    )
```

```python
import math

import ml_dtypes
import numpy as np
import jax
import jax.numpy as jnp
from jax import lax
from jax.experimental import pallas as pl
from jax.experimental.pallas import tpu as pltpu
from jax.sharding import PartitionSpec as P

BLK = 64
NV = 32
NC = 8
KS = 5
OMEGA = 2.0 / 3.0
MESH = pl.DeviceIdType.MESH
F32 = jnp.float32
BF16 = jnp.bfloat16

H = 16
W = 8
PW = W + 2
SPOTS = (H + 2) * PW
NB = 8
SENT1 = 5
SENT2 = 4

DIRS = [(1, 0), (-1, 0), (0, 1), (0, -1), (1, 1), (1, -1), (-1, 1), (-1, -1)]


def lanes(shape):
    return lax.broadcasted_iota(jnp.int32, shape, len(shape) - 1)


def sublanes(shape):
    return lax.broadcasted_iota(jnp.int32, shape, 0)


def lane_group(shape):
    return lanes(shape) // NV


def split2(x):
    hi = x.astype(BF16).astype(F32)
    return hi, x - hi


def split3(x):
    one = x.astype(BF16)
    rest = x - one.astype(F32)
    two = rest.astype(BF16)
    three = (rest - two.astype(F32)).astype(BF16)
    return one, two, three


def by_group(parts, group):
    out = parts[3]
    for n in (2, 1, 0):
        out = jnp.where(group == n, parts[n], out)
    return out


def body(n_slab, n_pencil, a_hbm, codes, agg_s, tv_hbm, modes_hbm, out_v, out_t, out_p,
         abuf, aprep, dinv, vf, pan0, pan1, wbuf, modes, copier, tv, vc, tmp, colsend, hrow, hcol, hcor,
         sq, send1, recv1, send2, recv2, xg, xedge, tiles, prods,
         a_sem, tv_sem, m_sem, o_sem, hs_sem, hr_sem, s1, r1, s2, r2):
    devices = n_slab * n_pencil
    slab = lax.axis_index("slab")
    pencil = lax.axis_index("pencil")
    me = slab * n_pencil + pencil

    def a_copy(i):
        return pltpu.make_async_copy(
            a_hbm.at[i], abuf.at[lax.rem(i, NB)], a_sem.at[lax.rem(i, NB)]
        )

    tv_copy = pltpu.make_async_copy(tv_hbm, tv, tv_sem)
    tv_copy.start()
    for i in range(NB):
        a_copy(i).start()

    m_copy = pltpu.make_async_copy(modes_hbm, modes, m_sem)
    m_copy.start()
    barrier = pltpu.get_barrier_semaphore()

    @pl.loop(1, devices)
    def _(n):
        d = lax.rem(me + n, devices)
        pl.semaphore_signal(
            barrier, inc=1, device_id=(d // n_pencil, lax.rem(d, n_pencil)), device_id_type=MESH
        )

    group16 = lane_group((16, 128))
    group64 = lane_group((64, 128))
    odd64 = lax.rem(group64, 2) == 1
    low64 = group64 < 2
    group32 = lane_group((32, 128))
    odd32 = lax.rem(group32, 2) == 1
    low32 = group32 < 2

    def spread(x, dst, *lead):
        turns = [x] + [pltpu.roll(x, NV * n, 1) for n in (1, 2, 3)]
        for s in range(4):
            dst[(*lead, pl.ds(s, 16, stride=4), slice(None))] = by_group(
                [turns[(g - s) % 4] for g in range(4)], group16
            )

    def panel_of(v):
        hi, lo = split2(v)
        w = jnp.where(odd64, lo, hi)
        both = jnp.concatenate([jnp.where(low64, w, 0.0), jnp.where(low64, 0.0, w)], axis=0)
        return both.astype(BF16)

    def gather_cells(b):
        return by_group([vf[b, pl.ds(s, 16, stride=4), :] for s in range(4)], group16)

    def remote(src, dst, rnd, n):
        ds, dp = DIRS[n]
        return pltpu.make_async_remote_copy(
            src_ref=src,
            dst_ref=dst,
            send_sem=hs_sem.at[rnd, n],
            recv_sem=hr_sem.at[rnd, n],
            device_id=(lax.rem(slab + ds + n_slab, n_slab), lax.rem(pencil + dp + n_pencil, n_pencil)),
            device_id_type=MESH,
        )

    def edge_copies(rnd, rows):
        copies = []
        for n, (ds, dp) in enumerate(DIRS):
            edge = (H - 1) if ds == 1 else 0
            if dp == 0:
                src, dst = rows.at[edge], hrow.at[rnd, n]
            elif ds == 0:
                src, dst = colsend.at[rnd, n - 2], hcol.at[rnd, n - 2]
            else:
                src = colsend.at[rnd, 0 if dp == 1 else 1, pl.ds(edge * 16, 16)]
                dst = hcor.at[rnd, n - 4]
            copies.append(remote(src, dst, rnd, n))
        return copies

    def from_inside(n):
        ds, dp = DIRS[n]
        ok_s = slab - ds
        ok_p = pencil - dp
        return jnp.logical_and(
            jnp.logical_and(ok_s >= 0, ok_s < n_slab), jnp.logical_and(ok_p >= 0, ok_p < n_pencil)
        )

    def take_edges(rnd, pan):
        for n, (ds, dp) in enumerate(DIRS):
            keep = from_inside(n).astype(F32)
            if dp == 0:
                base = 0 if ds == 1 else (H + 1) * PW
                for j in range(W):
                    spread(hrow[rnd, n, pl.ds(j, 16, stride=8), :] * keep, tmp, j)
                    pan[base + j + 1] = panel_of(tmp[j])
            elif ds == 0:
                col = 0 if dp == 1 else W + 1

                @pl.loop(0, H // 8)
                def _(q):
                    for u in range(8):
                        i = q * 8 + u
                        start = pl.multiple_of(i * 16, 16)
                        spread(hcol[rnd, n - 2, pl.ds(start, 16), :] * keep, tmp, u)
                        pan[(i + 1) * PW + col] = panel_of(tmp[u])
            else:
                spot = (0 if ds == 1 else H + 1) * PW + (0 if dp == 1 else W + 1)
                spread(hcor[rnd, n - 4] * keep, tmp, n)
                pan[spot] = panel_of(tmp[n])

    tv_copy.wait()
    for i in range(H):
        colsend[0, 0, i * 16:(i + 1) * 16, :] = tv[i, pl.ds(W - 1, 16, stride=8), :]
        colsend[0, 1, i * 16:(i + 1) * 16, :] = tv[i, pl.ds(0, 16, stride=8), :]

    @pl.loop(0, H)
    def _(i):
        for j in range(W):
            b = i * W + j
            spread(tv[i, pl.ds(j, 16, stride=8), :], vf, b)
            pan0[(i + 1) * PW + j + 1] = panel_of(vf[b])

    lane32 = lanes((32, 128))
    row32 = sublanes((32, 128))
    left = lane32 < 64
    on_even = lane32 == 2 * row32
    on_odd = lane32 == 2 * row32 + 65

    @pl.loop(0, H)
    def _(i):
        a_copy(i).wait()
        slot = lax.rem(i, NB)
        for j in range(W):
            b = i * W + j
            for k in range(KS):
                x = abuf[slot, pl.ds(k * 256 + j, 32, stride=8), :]
                hi = x.astype(BF16)
                lo = (x - hi.astype(F32)).astype(BF16)
                aprep[b * KS + k] = jnp.concatenate([hi, lo], axis=0)
                if k == 0:
                    d_even = jnp.sum(jnp.where(on_even, x, 0.0), axis=1, keepdims=True)
                    d_odd = jnp.sum(jnp.where(on_odd, x, 0.0), axis=1, keepdims=True)
                    dinv[b] = OMEGA / jnp.where(left, d_even, d_odd)

        @pl.when(i + NB < H)
        def _():
            a_copy(i + NB).start()

    lane_r = lanes((128, 128))
    row_r = sublanes((128, 128))
    for n in range(16):
        hit = row_r == n * NC + lax.rem(lane_r, NC)
        copier[:, n * 128:(n + 1) * 128] = jnp.where(hit, 1.0, 0.0).astype(BF16)

    def slot_spots(i, j):
        spots = []
        for k in range(KS):
            code = codes[k, j, i]
            di = (code * 11) >> 5
            spots.append((i + di) * PW + j + code - 3 * di)
        return spots

    def relax(cells, old, new, rnd, kept):
        images = []
        for i, j in cells:
            b = i * W + j
            left_side = jnp.concatenate([aprep[b * KS + k] for k in range(KS)], axis=1)
            right = jnp.concatenate([old[spot] for spot in slot_spots(i, j)], axis=0)
            images.append(jnp.dot(left_side, right, preferred_element_type=F32))
        for n, (i, j) in enumerate(cells):
            r = (images[n][0:32] + images[n][32:64]) * dinv[i * W + j]
            r1, r2, r3 = (pltpu.roll(r, NV * m, 1) for m in (1, 2, 3))
            sums = [r + r3, r + r1, r1 + r2, r2 + r3]
            tmp[n, pl.ds(0, 32, stride=2), :] = by_group(sums, group32)
            tmp[n, pl.ds(1, 32, stride=2), :] = by_group(sums[2:] + sums[:2], group32)
        fresh = [vf[i * W + j] - tmp[n] for n, (i, j) in enumerate(cells)]
        for v, (i, j) in zip(fresh, cells):
            vf[i * W + j] = v
        for v, (i, j) in zip(fresh, cells):
            new[(i + 1) * PW + j + 1] = panel_of(v)
        if kept:
            for n, (i, j) in enumerate(cells):
                keep_cells(i, j, rnd, n)

    def keep_cells(i, j, rnd, n):
        x = gather_cells(i * W + j)
        vc[i, pl.ds(j, 16, stride=8), :] = x
        if j in (0, W - 1):
            colsend[rnd, 0 if j else 1, pl.ds(pl.multiple_of(i * 16, 16), 16), :] = x
        if rnd == 2:
            sq[n] += x * x

    def inside(work, first=1, last=H - 1):
        @pl.loop(0, (last - first) // 2)
        def _(n):
            work([(first + 2 * n + u, j) for u in range(2) for j in range(1, W - 1)])

    def outside(work):
        @pl.loop(0, 2)
        def _(n):
            work([(1 + 7 * n + u, j) for u in range(7) for j in (0, W - 1)])

        @pl.loop(0, 2)
        def _(n):
            work([(n * (H - 1), j) for j in range(W)])

    def first(cells, kept):
        relax(cells, pan0, pan1, 1, kept)

    inside(lambda cells: first(cells, False), 1, 9)
    pl.semaphore_wait(barrier, devices - 1)
    edges0 = edge_copies(0, tv)
    for c in edges0:
        c.start()
    inside(lambda cells: first(cells, False), 9, 15)
    for c in edges0:
        c.wait()
    take_edges(0, pan0)
    outside(lambda cells: first(cells, True))
    edges1 = edge_copies(1, vc)
    for c in edges1:
        c.start()

    sq[...] = jnp.zeros_like(sq)

    def second(cells):
        relax(cells, pan1, pan0, 2, True)

    inside(second)
    for c in edges1:
        c.wait()
    take_edges(1, pan1)
    outside(second)
    edges2 = edge_copies(2, vc)
    for c in edges2:
        c.start()

    squares = sq[0]
    for n in range(1, 16):
        squares = squares + sq[n]
    squares = jnp.sum(squares, axis=0, keepdims=True)
    squares = squares + pltpu.roll(squares, 64, 1)
    squares = squares + pltpu.roll(squares, 32, 1)

    lane_d = lanes((devices, 128))
    row_d = sublanes((devices, 128))
    group_d = lane_d // NV
    lane1 = lanes((1, 128))
    rows = []
    for j in range(W):
        row = jnp.zeros((1, 128), jnp.int32)
        for i in range(H):
            row = jnp.where(lane1 == i * W + j, agg_s[j, i], row)
        rows.append(row)
    while len(rows) > 1:
        rows = [x + y for x, y in zip(rows[::2], rows[1::2])]
    agg = rows[0]
    mine = jnp.broadcast_to(agg >> 4, (devices, 128)) == row_d
    local = jnp.broadcast_to((agg & 15) + 1, (devices, 128)).astype(F32)
    parity = lane_d & 1
    m_copy.wait()
    coef = jnp.zeros((H * W, 2 * 128), F32)
    for q in range(16):
        x = jnp.concatenate([vc[i, q * 8:(q + 1) * 8, :] for i in range(H)], axis=0)
        hi, lo = split2(x)
        coef = coef + jnp.dot(
            jnp.concatenate([hi, lo, hi], axis=1).astype(BF16),
            jnp.concatenate([modes[q, 0:128], modes[q]], axis=0),
            preferred_element_type=F32,
        )
    parts = jnp.concatenate(split3(coef), axis=0)
    fifth = jnp.broadcast_to(squares, (devices, 128))
    for cap in range(2):
        chosen = jnp.logical_and(mine, parity == cap).astype(F32)
        chosen_b = chosen.astype(BF16)
        packed = jnp.dot(
            jnp.concatenate([chosen_b] * 3, axis=1), parts, preferred_element_type=F32
        )
        send1[pl.ds(2 * cap, devices, stride=8), :] = packed[:, 0:128]
        send1[pl.ds(2 * cap + 1, devices, stride=8), :] = packed[:, 128:256]
        ident = jnp.sum(chosen * local, axis=1, keepdims=True)
        fifth = jnp.where(group_d == cap + 1, ident, fifth)
    send1[pl.ds(4, devices, stride=8), :] = fifth

    my_start = pl.multiple_of(me * 8, 8)

    @pl.loop(1, devices)
    def _(n):
        d = lax.rem(me + n, devices)
        pltpu.make_async_remote_copy(
            src_ref=send1.at[pl.ds(pl.multiple_of(d * 8, 8), SENT1)],
            dst_ref=recv1.at[pl.ds(my_start, SENT1)],
            send_sem=s1,
            recv_sem=r1,
            device_id=(d // n_pencil, lax.rem(d, n_pencil)),
            device_id_type=MESH,
        ).start()

    own1 = pltpu.make_async_copy(
        send1.at[pl.ds(my_start, SENT1)], recv1.at[pl.ds(my_start, SENT1)], r1
    )
    own1.start()

    def image_of(cells):
        for i, j in cells:
            b = i * W + j
            spots = slot_spots(i, j)
            for k in range(KS + 1):
                if k < KS:
                    o = jnp.dot(aprep[b * KS + k], pan0[spots[k]], preferred_element_type=F32)
                    r = o[0:32] + o[32:64]
                    z = r + jnp.where(odd32, pltpu.roll(r, NV, 1), pltpu.roll(r, 128 - NV, 1))
                else:
                    z = jnp.where(
                        low32, vf[b, pl.ds(0, 32, stride=2), :], vf[b, pl.ds(1, 32, stride=2), :]
                    )
                hi, lo = split2(z)
                wbuf[b * (KS + 1) + k] = jnp.where(odd32, lo, hi).astype(BF16)

    inside(image_of)

    pltpu.make_async_copy(
        send1.at[pl.ds(0, devices * SENT1)], recv1.at[pl.ds(0, devices * SENT1)], r1
    ).wait()

    heard = recv1[pl.ds(4, devices, stride=8), :]
    total = jnp.sum(heard, axis=0, keepdims=True)
    total = jnp.where(lane1 < NV, total, 0.0)
    total = total + pltpu.roll(total, 64, 1)
    total = total + pltpu.roll(total, 32, 1)
    inv = 1.0 / jnp.sqrt(total / (H * W * BLK * devices) + 1e-06)

    want = (lane_d + 1).astype(F32)
    few = lane_d < 16
    member_t = [
        jnp.where(jnp.logical_and(pltpu.roll(heard, 128 - NV * (cap + 1), 1) == want, few), 1.0, 0.0)
        for cap in range(2)
    ]
    member = [m.T[0:16] for m in member_t]
    counts = jnp.sum(member[0] + member[1], axis=1, keepdims=True)
    lhs, rhs = [], []
    for cap in range(2):
        rows = jnp.concatenate(
            [recv1[pl.ds(2 * cap + h, devices, stride=8), :] for h in range(2)], axis=1
        )
        lhs += [member[cap].astype(BF16)] * 3
        rhs += list(split3(rows))
    coarse = jnp.dot(
        jnp.concatenate(lhs, axis=1), jnp.concatenate(rhs, axis=0), preferred_element_type=F32
    )
    coarse = coarse * jnp.concatenate([inv, inv], axis=1) / jnp.maximum(counts, 1.0)
    in_first = lanes((16, 128)) < NV
    fit = []
    for k in range(NC):
        half = coarse[:, 128 * (k // 4):128 * (k // 4) + 128]
        if k % 4:
            half = pltpu.roll(half, 128 - NV * (k % 4), 1)
        fit.append(jnp.where(in_first, half, 0.0))
    gram = {}
    for k in range(NC):
        for l in range(k + 1):
            gram[k, l] = jnp.sum(fit[k] * fit[l], axis=1, keepdims=True)
    trace_sum = gram[0, 0]
    for k in range(1, NC):
        trace_sum = trace_sum + gram[k, k]
    ridge = 0.1 * trace_sum / NC + 1e-06
    low, raw, pivot = {}, {}, {}
    for k in range(NC):
        top = gram[k, k] + ridge
        for l in range(k):
            top = top - raw[k, l] * low[k, l]
        pivot[k] = 1.0 / top
        for m in range(k + 1, NC):
            val = gram[m, k]
            for l in range(k):
                val = val - raw[m, l] * low[k, l]
            raw[m, k] = val
            low[m, k] = val * pivot[k]
    sol = []
    for k in range(NC):
        y = fit[k]
        for l in range(k):
            y = y - low[k, l] * sol[l]
        sol.append(y)
    for k in range(NC):
        sol[k] = sol[k] * pivot[k]
    for k in reversed(range(NC)):
        for l in range(k + 1, NC):
            sol[k] = sol[k] - low[l, k] * sol[l]
    columns = []
    for r in range(SENT2):
        pair = sol[r] * inv + pltpu.roll(sol[r + 4] * inv, 64, 1)
        columns.append(jnp.concatenate([pair, pltpu.roll(pair, NV, 1)], axis=0))
    pieces = list(split3(jnp.concatenate(columns, axis=1)))
    table = jnp.concatenate(pieces + [jnp.zeros_like(pieces[0])], axis=0)
    pick = member_t[0] + pltpu.roll(member_t[1], 16, 1)
    pick = pick + pltpu.roll(pick, 32, 1) + pltpu.roll(pick, 64, 1)
    replies = jnp.dot(pick.astype(BF16), table, preferred_element_type=F32)
    for r in range(SENT2):
        send2[pl.ds(r, devices, stride=8), :] = replies[:, 128 * r:128 * (r + 1)]

    @pl.loop(1, devices)
    def _(n):
        d = lax.rem(me + n, devices)
        pltpu.make_async_remote_copy(
            src_ref=send2.at[pl.ds(pl.multiple_of(d * 8, 8), SENT2)],
            dst_ref=recv2.at[me, pl.ds(0, SENT2)],
            send_sem=s2,
            recv_sem=r2,
            device_id=(d // n_pencil, lax.rem(d, n_pencil)),
            device_id_type=MESH,
        ).start()

    own2 = pltpu.make_async_copy(
        send2.at[pl.ds(my_start, SENT2)], recv2.at[me, pl.ds(0, SENT2)], r2
    )
    own2.start()

    for c in edges2:
        c.wait()
    take_edges(2, pan0)
    outside(image_of)

    @pl.loop(0, H)
    def _(i):
        vc[i] = vc[i] * inv

    v_copy = pltpu.make_async_copy(vc, out_v, o_sem.at[0])
    v_copy.start()
    pltpu.make_async_copy(
        recv1.at[pl.ds(0, devices * SENT2)], recv1.at[pl.ds(0, devices * SENT2)], r2
    ).wait()

    group8 = lane_group((8, 128))
    low8 = group8 < 2
    sub8 = sublanes((8, 128))

    @pl.loop(0, H)
    def _(i):
        for g in range(W // 2):
            x = recv2[agg_s[2 * g, i] >> 4]
            x = jnp.where(sub8 < 4, x, pltpu.roll(pltpu.roll(x, 4, 0), 64, 1))
            xg[i, g] = x

    edges3 = []
    for n, (ds, dp) in enumerate(DIRS):
        edge = (H - 1) if ds == 1 else 0
        side = (W // 2 - 1) if dp == 1 else 0
        if dp == 0:
            edges3.append(remote(xg.at[edge], xedge.at[pl.ds(4 * n, 4)], 3, n))
        elif ds == 0:
            edges3.append(
                remote(xg.at[:, side], xedge.at[pl.ds(8 + 16 * (n - 2), H)], 3, n)
            )
        else:
            edges3.append(remote(xg.at[edge, side], xedge.at[40 + n - 4], 3, n))
    for c in edges3:
        c.start()

    even_cell = lax.rem(lanes((32, 128)) // NC, 2) == 0
    xw = pan1

    def fit_weights(fits, places):
        t = fits.T[0:64]
        pieces = jnp.concatenate(split2(t), axis=0).astype(BF16)
        for n in range(8):
            o = jnp.dot(pieces, copier[:, n * 256:(n + 1) * 256], preferred_element_type=F32)
            for u in range(2):
                for cap in range(2):
                    place = places[2 * n + u][cap]
                    if place is None:
                        continue
                    parts = []
                    for p in range(2):
                        x = o[64 * p + 32 * cap:64 * p + 32 * cap + 32, 128 * u:128 * u + 128]
                        parts += [jnp.where(even_cell, x, 0.0), jnp.where(even_cell, 0.0, x)]
                    xw[place] = jnp.concatenate(parts, axis=0).astype(BF16)

    @pl.loop(0, 2)
    def _(n):
        for h in range(2):
            i0 = n * 8 + h * 4
            fits = jnp.concatenate([xg[i0 + u, g] for u in range(4) for g in range(W // 2)], axis=0)
            fit_weights(
                fits,
                [
                    [(i0 + u + 1) * PW + 2 * g + cap + 1 for cap in range(2)]
                    for u in range(4)
                    for g in range(W // 2)
                ],
            )

    lane_q = lanes((8, 128)) // 16
    even_s = lax.rem(sub8, 2) == 0
    two_s = lax.rem(sub8 // 2, 2) == 0
    keep1 = lax.rem(lane_q, 2) == lax.rem(sub8, 2)
    at1 = jnp.where(keep1, lane_q, lax.rem(lane_q + 1, 8))
    keep2 = lax.rem(at1 // 2, 2) == lax.rem(sub8 // 2, 2)
    at2 = jnp.where(keep2, at1, lax.rem(at1 + 2, 8))
    keep3 = at2 == sub8

    def own_rows(s):
        z = [s[8 * r:8 * r + 8] for r in range(4)]

        def merge(x, y, first, keep, shift):
            return jnp.where(
                keep, jnp.where(first, x, y), pltpu.roll(jnp.where(first, y, x), shift, 0)
            )

        u = merge(
            merge(z[0], z[1], even_s, keep1, 1), merge(z[2], z[3], even_s, keep1, 1), two_s, keep2, 2
        )
        return jnp.where(keep3, u, pltpu.roll(u, 4, 0))[0:4]

    def finish(cells):
        for i, j in cells:
            b = i * W + j
            spots = slot_spots(i, j) + [(i + 1) * PW + j + 1]
            for k in range(KS + 1):
                w = wbuf[b * (KS + 1) + k]
                x = [xw[spots[k], 32 * m:32 * m + 32] for m in range(4)]
                s = jnp.dot(
                    jnp.concatenate([w, w], axis=1),
                    jnp.concatenate([x[m // 2] for m in range(8)], axis=0),
                    preferred_element_type=F32,
                )
                if k < KS:
                    prods[i, pl.ds(k * 32 + j, 4, stride=8), :] = own_rows(s)
                else:
                    tiles[i, pl.ds(j, 4, stride=8), :] = own_rows(s)

    inside(finish)
    for c in edges3:
        c.wait()
    places = [[None, None] for _ in range(44)]
    for n, (ds, dp) in enumerate(DIRS):
        row = (0 if ds == 1 else H + 1) * PW
        col = 0 if dp == 1 else W + 1
        cap = 1 if dp == 1 else 0
        if dp == 0:
            for j in range(W):
                places[4 * n + j // 2][j % 2] = row + j + 1
        elif ds == 0:
            for i in range(H):
                places[8 + 16 * (n - 2) + i][cap] = (i + 1) * PW + col
        else:
            places[40 + n - 4][cap] = row + col
    for n in range(3):
        tiles16 = [xedge[16 * n + u] for u in range(16 if n < 2 else 12)]
        tiles16 += [jnp.zeros((8, 128), F32)] * (16 - len(tiles16))
        fit_weights(
            jnp.concatenate(tiles16, axis=0), (places + [[None, None]] * 4)[16 * n:16 * n + 16]
        )
    outside(finish)
    t_copy = pltpu.make_async_copy(tiles, out_t, o_sem.at[1])
    p_copy = pltpu.make_async_copy(prods, out_p, o_sem.at[2])
    t_copy.start()
    p_copy.start()

    def sent(rows, sem):
        part = recv1.at[pl.ds(0, (devices - 1) * rows)]
        pltpu.make_async_copy(part, part, sem).wait()

    sent(SENT1, s1)
    sent(SENT2, s2)
    v_copy.wait()
    t_copy.wait()
    p_copy.wait()


def mode_blocks():
    centre = np.arange(BLK, dtype=np.float64) + 0.5
    table = np.cos(math.pi * centre[:, None] * np.arange(NC)[None, :] / BLK).astype(np.float32)
    dense = np.einsum("qsm,vw->qsvmw", table.reshape(16, 4, NC), np.eye(NV, dtype=np.float32))
    dense = dense.reshape(16, 4 * NV, NC * NV)
    hi = dense.astype(ml_dtypes.bfloat16)
    lo = (dense - hi.astype(np.float32)).astype(ml_dtypes.bfloat16)
    return np.concatenate([hi, lo], axis=1)


def solution(mesh):
    n_slab = mesh.shape["slab"]
    n_pencil = mesh.shape["pencil"]
    devices = n_slab * n_pencil

    def shards(a_blocks, col_codes, agg_of, test_vectors):
        a = a_blocks.reshape(H, W, 160, 128).transpose(0, 2, 1, 3).reshape(H, 1280, 128)
        tv = test_vectors.reshape(H, W, 16, 128).transpose(0, 2, 1, 3).reshape(H, 128, 128)
        vmem = pl.BlockSpec(memory_space=pltpu.VMEM)
        smem = pl.BlockSpec(memory_space=pltpu.SMEM)
        hbm = pl.BlockSpec(memory_space=pl.ANY)
        dma = pltpu.SemaphoreType.DMA
        out_v, out_t, out_p = pl.pallas_call(
            lambda *refs: body(n_slab, n_pencil, *refs),
            out_shape=(
                jax.ShapeDtypeStruct((H, 128, 128), F32),
                jax.ShapeDtypeStruct((H, 32, 128), F32),
                jax.ShapeDtypeStruct((H, 160, 128), F32),
            ),
            in_specs=[hbm, smem, smem, hbm, hbm],
            out_specs=(hbm, hbm, hbm),
            scratch_shapes=[
                pltpu.VMEM((NB, 1280, 128), F32),
                pltpu.VMEM((H * W * KS, 64, 128), BF16),
                pltpu.VMEM((H * W, 32, 128), F32),
                pltpu.VMEM((H * W, 64, 128), F32),
                pltpu.VMEM((SPOTS, 128, 128), BF16),
                pltpu.VMEM((SPOTS, 128, 128), BF16),
                pltpu.VMEM((H * W * (KS + 1), 32, 128), BF16),
                pltpu.VMEM((16, 256, 256), BF16),
                pltpu.VMEM((128, 2048), BF16),
                pltpu.VMEM((H, 128, 128), F32),
                pltpu.VMEM((H, 128, 128), F32),
                pltpu.VMEM((16, 64, 128), F32),
                pltpu.VMEM((3, 2, 256, 128), F32),
                pltpu.VMEM((3, 2, 128, 128), F32),
                pltpu.VMEM((3, 2, 256, 128), F32),
                pltpu.VMEM((3, 4, 16, 128), F32),
                pltpu.VMEM((16, 16, 128), F32),
                pltpu.VMEM((devices * 8, 128), F32),
                pltpu.VMEM((devices * 8, 128), F32),
                pltpu.VMEM((devices * 8, 128), F32),
                pltpu.VMEM((devices, 8, 128), F32),
                pltpu.VMEM((H, W // 2, 8, 128), F32),
                pltpu.VMEM((44, 8, 128), F32),
                pltpu.VMEM((H, 32, 128), F32),
                pltpu.VMEM((H, 160, 128), F32),
                dma((NB,)),
                dma,
                dma,
                dma((3,)),
                dma((4, 8)),
                dma((4, 8)),
                dma,
                dma,
                dma,
                dma,
            ],
            compiler_params=pltpu.CompilerParams(
                collective_id=0, has_side_effects=True, vmem_limit_bytes=60 * 1024 * 1024
            ),
        )(a, col_codes.transpose(2, 1, 0), agg_of.T, tv, jnp.asarray(mode_blocks()))
        relaxed = out_v.reshape(H, 16, W, 128).transpose(0, 2, 1, 3).reshape(H, W, BLK * NV)
        tiles = out_t.reshape(H, 4, W, 128).transpose(0, 2, 1, 3).reshape(H, W, BLK * NC)
        products = out_p.reshape(H, 20, W, 128).transpose(0, 2, 1, 3).reshape(H, W, KS * BLK * NC)
        return relaxed, tiles, products

    spec = P("slab", "pencil", None)
    return jax.shard_map(
        shards,
        mesh=mesh,
        in_specs=(spec, spec, P("slab", "pencil"), spec),
        out_specs=(spec, spec, spec),
        check_vma=False,
    )
```

```python
import math

import ml_dtypes
import numpy as np
import jax
import jax.numpy as jnp
from jax import lax
from jax.experimental import pallas as pl
from jax.experimental.pallas import tpu as pltpu
from jax.sharding import PartitionSpec as P

BLK = 64
NV = 32
NC = 8
KS = 5
OMEGA = 2.0 / 3.0
MESH = pl.DeviceIdType.MESH
F32 = jnp.float32
BF16 = jnp.bfloat16

H = 16
W = 8
PW = W + 2
SPOTS = (H + 2) * PW
NB = 8
SENT1 = 5
SENT2 = 4

DIRS = [(1, 0), (-1, 0), (0, 1), (0, -1), (1, 1), (1, -1), (-1, 1), (-1, -1)]


def lanes(shape):
    return lax.broadcasted_iota(jnp.int32, shape, len(shape) - 1)


def sublanes(shape):
    return lax.broadcasted_iota(jnp.int32, shape, 0)


def lane_group(shape):
    return lanes(shape) // NV


def split2(x):
    hi = x.astype(BF16).astype(F32)
    return hi, x - hi


def split3(x):
    one = x.astype(BF16)
    rest = x - one.astype(F32)
    two = rest.astype(BF16)
    three = (rest - two.astype(F32)).astype(BF16)
    return one, two, three


def by_group(parts, group):
    out = parts[3]
    for n in (2, 1, 0):
        out = jnp.where(group == n, parts[n], out)
    return out


def body(n_slab, n_pencil, a_hbm, codes, agg_s, tv_hbm, modes_hbm, out_v, out_t, out_p,
         abuf, aprep, dinv, vf, pan0, pan1, wbuf, modes, copier, tv, vc, tmp, colsend, hrow, hcol, hcor,
         sq, send1, recv1, send2, recv2, xg, xedge, tiles, prods,
         a_sem, tv_sem, m_sem, o_sem, hs_sem, hr_sem, s1, r1, s2, r2):
    devices = n_slab * n_pencil
    slab = lax.axis_index("slab")
    pencil = lax.axis_index("pencil")
    me = slab * n_pencil + pencil

    def a_copy(i):
        return pltpu.make_async_copy(
            a_hbm.at[i], abuf.at[lax.rem(i, NB)], a_sem.at[lax.rem(i, NB)]
        )

    tv_copy = pltpu.make_async_copy(tv_hbm, tv, tv_sem)
    tv_copy.start()
    for i in range(NB):
        a_copy(i).start()

    m_copy = pltpu.make_async_copy(modes_hbm, modes, m_sem)
    m_copy.start()
    barrier = pltpu.get_barrier_semaphore()

    @pl.loop(1, devices)
    def _(n):
        d = lax.rem(me + n, devices)
        pl.semaphore_signal(
            barrier, inc=1, device_id=(d // n_pencil, lax.rem(d, n_pencil)), device_id_type=MESH
        )

    group16 = lane_group((16, 128))
    group64 = lane_group((64, 128))
    odd64 = lax.rem(group64, 2) == 1
    low64 = group64 < 2
    group32 = lane_group((32, 128))
    odd32 = lax.rem(group32, 2) == 1
    low32 = group32 < 2

    def spread(x, dst, *lead):
        turns = [x] + [pltpu.roll(x, NV * n, 1) for n in (1, 2, 3)]
        for s in range(4):
            dst[(*lead, pl.ds(s, 16, stride=4), slice(None))] = by_group(
                [turns[(g - s) % 4] for g in range(4)], group16
            )

    def panel_of(v):
        hi, lo = split2(v)
        w = jnp.where(odd64, lo, hi)
        both = jnp.concatenate([jnp.where(low64, w, 0.0), jnp.where(low64, 0.0, w)], axis=0)
        return both.astype(BF16)

    def gather_cells(b):
        return by_group([vf[b, pl.ds(s, 16, stride=4), :] for s in range(4)], group16)

    def remote(src, dst, rnd, n):
        ds, dp = DIRS[n]
        return pltpu.make_async_remote_copy(
            src_ref=src,
            dst_ref=dst,
            send_sem=hs_sem.at[rnd, n],
            recv_sem=hr_sem.at[rnd, n],
            device_id=(lax.rem(slab + ds + n_slab, n_slab), lax.rem(pencil + dp + n_pencil, n_pencil)),
            device_id_type=MESH,
        )

    def edge_copies(rnd, rows):
        copies = []
        for n, (ds, dp) in enumerate(DIRS):
            edge = (H - 1) if ds == 1 else 0
            if dp == 0:
                src, dst = rows.at[edge], hrow.at[rnd, n]
            elif ds == 0:
                src, dst = colsend.at[rnd, n - 2], hcol.at[rnd, n - 2]
            else:
                src = colsend.at[rnd, 0 if dp == 1 else 1, pl.ds(edge * 16, 16)]
                dst = hcor.at[rnd, n - 4]
            copies.append(remote(src, dst, rnd, n))
        return copies

    def from_inside(n):
        ds, dp = DIRS[n]
        ok_s = slab - ds
        ok_p = pencil - dp
        return jnp.logical_and(
            jnp.logical_and(ok_s >= 0, ok_s < n_slab), jnp.logical_and(ok_p >= 0, ok_p < n_pencil)
        )

    def take_edges(rnd, pan):
        for n, (ds, dp) in enumerate(DIRS):
            keep = from_inside(n).astype(F32)
            if dp == 0:
                base = 0 if ds == 1 else (H + 1) * PW
                for j in range(W):
                    spread(hrow[rnd, n, pl.ds(j, 16, stride=8), :] * keep, tmp, n * W + j)
                for j in range(W):
                    pan[base + j + 1] = panel_of(tmp[n * W + j])
            elif ds == 0:
                col = 0 if dp == 1 else W + 1

                for i in range(H):
                    spread(hcol[rnd, n - 2, i * 16:(i + 1) * 16, :] * keep, tmp, i)
                for i in range(H):
                    pan[(i + 1) * PW + col] = panel_of(tmp[i])
            else:
                spot = (0 if ds == 1 else H + 1) * PW + (0 if dp == 1 else W + 1)
                spread(hcor[rnd, n - 4] * keep, tmp, n)
                pan[spot] = panel_of(tmp[n])

    tv_copy.wait()
    for i in range(H):
        colsend[0, 0, i * 16:(i + 1) * 16, :] = tv[i, pl.ds(W - 1, 16, stride=8), :]
        colsend[0, 1, i * 16:(i + 1) * 16, :] = tv[i, pl.ds(0, 16, stride=8), :]

    @pl.loop(0, H)
    def _(i):
        for j in range(W):
            b = i * W + j
            spread(tv[i, pl.ds(j, 16, stride=8), :], vf, b)
            pan0[(i + 1) * PW + j + 1] = panel_of(vf[b])

    lane32 = lanes((32, 128))
    row32 = sublanes((32, 128))
    left = lane32 < 64
    on_even = lane32 == 2 * row32
    on_odd = lane32 == 2 * row32 + 65

    @pl.loop(0, H)
    def _(i):
        a_copy(i).wait()
        slot = lax.rem(i, NB)
        for j in range(W):
            b = i * W + j
            for k in range(KS):
                x = abuf[slot, pl.ds(k * 256 + j, 32, stride=8), :]
                hi = x.astype(BF16)
                lo = (x - hi.astype(F32)).astype(BF16)
                aprep[b * KS + k] = jnp.concatenate([hi, lo], axis=0)
                if k == 0:
                    d_even = jnp.sum(jnp.where(on_even, x, 0.0), axis=1, keepdims=True)
                    d_odd = jnp.sum(jnp.where(on_odd, x, 0.0), axis=1, keepdims=True)
                    dinv[b] = OMEGA / jnp.where(left, d_even, d_odd)

        @pl.when(i + NB < H)
        def _():
            a_copy(i + NB).start()

    lane_r = lanes((128, 128))
    row_r = sublanes((128, 128))
    for n in range(16):
        hit = row_r == n * NC + lax.rem(lane_r, NC)
        copier[:, n * 128:(n + 1) * 128] = jnp.where(hit, 1.0, 0.0).astype(BF16)

    def slot_spots(i, j):
        spots = []
        for k in range(KS):
            code = codes[k, j, i]
            di = (code * 11) >> 5
            spots.append((i + di) * PW + j + code - 3 * di)
        return spots

    def relax(cells, old, new, rnd, kept):
        images = []
        for i, j in cells:
            b = i * W + j
            left_side = jnp.concatenate([aprep[b * KS + k] for k in range(KS)], axis=1)
            right = jnp.concatenate([old[spot] for spot in slot_spots(i, j)], axis=0)
            images.append(jnp.dot(left_side, right, preferred_element_type=F32))
        for n, (i, j) in enumerate(cells):
            r = (images[n][0:32] + images[n][32:64]) * dinv[i * W + j]
            r1, r2, r3 = (pltpu.roll(r, NV * m, 1) for m in (1, 2, 3))
            sums = [r + r3, r + r1, r1 + r2, r2 + r3]
            tmp[n, pl.ds(0, 32, stride=2), :] = by_group(sums, group32)
            tmp[n, pl.ds(1, 32, stride=2), :] = by_group(sums[2:] + sums[:2], group32)
        fresh = [vf[i * W + j] - tmp[n] for n, (i, j) in enumerate(cells)]
        for v, (i, j) in zip(fresh, cells):
            vf[i * W + j] = v
        for v, (i, j) in zip(fresh, cells):
            new[(i + 1) * PW + j + 1] = panel_of(v)
        if kept:
            for n, (i, j) in enumerate(cells):
                keep_cells(i, j, rnd, n)

    def keep_cells(i, j, rnd, n):
        x = gather_cells(i * W + j)
        vc[i, pl.ds(j, 16, stride=8), :] = x
        if j in (0, W - 1):
            colsend[rnd, 0 if j else 1, pl.ds(pl.multiple_of(i * 16, 16), 16), :] = x
        if rnd == 2:
            sq[n] += x * x

    def inside(work, first=1, last=H - 1):
        @pl.loop(0, (last - first) // 2)
        def _(n):
            work([(first + 2 * n + u, j) for u in range(2) for j in range(1, W - 1)])

    def outside(work):
        @pl.loop(0, 2)
        def _(n):
            work([(1 + 7 * n + u, j) for u in range(7) for j in (0, W - 1)])

        work([(i, j) for i in (0, H - 1) for j in range(W)])

    def first(cells, kept):
        relax(cells, pan0, pan1, 1, kept)

    inside(lambda cells: first(cells, False), 1, 9)
    pl.semaphore_wait(barrier, devices - 1)
    edges0 = edge_copies(0, tv)
    for c in edges0:
        c.start()
    inside(lambda cells: first(cells, False), 9, 15)
    for c in edges0:
        c.wait()
    take_edges(0, pan0)
    outside(lambda cells: first(cells, True))
    edges1 = edge_copies(1, vc)
    for c in edges1:
        c.start()

    sq[...] = jnp.zeros_like(sq)

    def again(cells):
        relax(cells, pan1, pan0, 2, True)

    inside(again)
    for c in edges1:
        c.wait()
    take_edges(1, pan1)
    outside(again)
    edges2 = edge_copies(2, vc)
    for c in edges2:
        c.start()

    squares = sq[0]
    for n in range(1, 16):
        squares = squares + sq[n]
    squares = jnp.sum(squares, axis=0, keepdims=True)
    squares = squares + pltpu.roll(squares, 64, 1)
    squares = squares + pltpu.roll(squares, 32, 1)

    lane_d = lanes((devices, 128))
    row_d = sublanes((devices, 128))
    group_d = lane_d // NV
    lane1 = lanes((1, 128))
    rows = []
    for j in range(W):
        row = jnp.zeros((1, 128), jnp.int32)
        for i in range(H):
            row = jnp.where(lane1 == i * W + j, agg_s[j, i], row)
        rows.append(row)
    while len(rows) > 1:
        rows = [x + y for x, y in zip(rows[::2], rows[1::2])]
    agg = rows[0]
    mine = jnp.broadcast_to(agg >> 4, (devices, 128)) == row_d
    local = jnp.broadcast_to((agg & 15) + 1, (devices, 128)).astype(F32)
    parity = lane_d & 1
    m_copy.wait()
    coef = jnp.zeros((H * W, 2 * 128), F32)
    for q in range(16):
        x = jnp.concatenate([vc[i, q * 8:(q + 1) * 8, :] for i in range(H)], axis=0)
        hi, lo = split2(x)
        coef = coef + jnp.dot(
            jnp.concatenate([hi, lo, hi], axis=1).astype(BF16),
            jnp.concatenate([modes[q, 0:128], modes[q]], axis=0),
            preferred_element_type=F32,
        )
    parts = jnp.concatenate(split3(coef), axis=0)
    fifth = jnp.broadcast_to(squares, (devices, 128))
    for cap in range(2):
        chosen = jnp.logical_and(mine, parity == cap).astype(F32)
        chosen_b = chosen.astype(BF16)
        packed = jnp.dot(
            jnp.concatenate([chosen_b] * 3, axis=1), parts, preferred_element_type=F32
        )
        send1[pl.ds(2 * cap, devices, stride=8), :] = packed[:, 0:128]
        send1[pl.ds(2 * cap + 1, devices, stride=8), :] = packed[:, 128:256]
        ident = jnp.sum(chosen * local, axis=1, keepdims=True)
        fifth = jnp.where(group_d == cap + 1, ident, fifth)
    send1[pl.ds(4, devices, stride=8), :] = fifth

    my_start = pl.multiple_of(me * 8, 8)

    @pl.loop(1, devices)
    def _(n):
        d = lax.rem(me + n, devices)
        pltpu.make_async_remote_copy(
            src_ref=send1.at[pl.ds(pl.multiple_of(d * 8, 8), SENT1)],
            dst_ref=recv1.at[pl.ds(my_start, SENT1)],
            send_sem=s1,
            recv_sem=r1,
            device_id=(d // n_pencil, lax.rem(d, n_pencil)),
            device_id_type=MESH,
        ).start()

    own1 = pltpu.make_async_copy(
        send1.at[pl.ds(my_start, SENT1)], recv1.at[pl.ds(my_start, SENT1)], r1
    )
    own1.start()

    def image_of(cells):
        for i, j in cells:
            b = i * W + j
            spots = slot_spots(i, j)
            for k in range(KS + 1):
                if k < KS:
                    o = jnp.dot(aprep[b * KS + k], pan0[spots[k]], preferred_element_type=F32)
                    r = o[0:32] + o[32:64]
                    z = r + jnp.where(odd32, pltpu.roll(r, NV, 1), pltpu.roll(r, 128 - NV, 1))
                else:
                    z = jnp.where(
                        low32, vf[b, pl.ds(0, 32, stride=2), :], vf[b, pl.ds(1, 32, stride=2), :]
                    )
                hi, lo = split2(z)
                wbuf[b * (KS + 1) + k] = jnp.where(odd32, lo, hi).astype(BF16)

    inside(image_of)

    pltpu.make_async_copy(
        send1.at[pl.ds(0, devices * SENT1)], recv1.at[pl.ds(0, devices * SENT1)], r1
    ).wait()

    heard = recv1[pl.ds(4, devices, stride=8), :]
    total = jnp.sum(heard, axis=0, keepdims=True)
    total = jnp.where(lane1 < NV, total, 0.0)
    total = total + pltpu.roll(total, 64, 1)
    total = total + pltpu.roll(total, 32, 1)
    inv = 1.0 / jnp.sqrt(total / (H * W * BLK * devices) + 1e-06)

    want = (lane_d + 1).astype(F32)
    few = lane_d < 16
    member_t = [
        jnp.where(jnp.logical_and(pltpu.roll(heard, 128 - NV * (cap + 1), 1) == want, few), 1.0, 0.0)
        for cap in range(2)
    ]
    member = [m.T[0:16] for m in member_t]
    counts = jnp.sum(member[0] + member[1], axis=1, keepdims=True)
    lhs, rhs = [], []
    for cap in range(2):
        rows = jnp.concatenate(
            [recv1[pl.ds(2 * cap + h, devices, stride=8), :] for h in range(2)], axis=1
        )
        lhs += [member[cap].astype(BF16)] * 3
        rhs += list(split3(rows))
    coarse = jnp.dot(
        jnp.concatenate(lhs, axis=1), jnp.concatenate(rhs, axis=0), preferred_element_type=F32
    )
    coarse = coarse * jnp.concatenate([inv, inv], axis=1) / jnp.maximum(counts, 1.0)
    in_first = lanes((16, 128)) < NV
    fit = []
    for k in range(NC):
        half = coarse[:, 128 * (k // 4):128 * (k // 4) + 128]
        if k % 4:
            half = pltpu.roll(half, 128 - NV * (k % 4), 1)
        fit.append(jnp.where(in_first, half, 0.0))
    gram = {}
    for k in range(NC):
        for l in range(k + 1):
            gram[k, l] = jnp.sum(fit[k] * fit[l], axis=1, keepdims=True)
    trace_sum = gram[0, 0]
    for k in range(1, NC):
        trace_sum = trace_sum + gram[k, k]
    ridge = 0.1 * trace_sum / NC + 1e-06
    low, raw, pivot = {}, {}, {}
    for k in range(NC):
        top = gram[k, k] + ridge
        for l in range(k):
            top = top - raw[k, l] * low[k, l]
        pivot[k] = 1.0 / top
        for m in range(k + 1, NC):
            val = gram[m, k]
            for l in range(k):
                val = val - raw[m, l] * low[k, l]
            raw[m, k] = val
            low[m, k] = val * pivot[k]
    sol = []
    for k in range(NC):
        y = fit[k]
        for l in range(k):
            y = y - low[k, l] * sol[l]
        sol.append(y)
    for k in range(NC):
        sol[k] = sol[k] * pivot[k]
    for k in reversed(range(NC)):
        for l in range(k + 1, NC):
            sol[k] = sol[k] - low[l, k] * sol[l]
    columns = []
    for r in range(SENT2):
        pair = sol[r] * inv + pltpu.roll(sol[r + 4] * inv, 64, 1)
        columns.append(jnp.concatenate([pair, pltpu.roll(pair, NV, 1)], axis=0))
    pieces = list(split3(jnp.concatenate(columns, axis=1)))
    table = jnp.concatenate(pieces + [jnp.zeros_like(pieces[0])], axis=0)
    pick = member_t[0] + pltpu.roll(member_t[1], 16, 1)
    pick = pick + pltpu.roll(pick, 32, 1) + pltpu.roll(pick, 64, 1)
    replies = jnp.dot(pick.astype(BF16), table, preferred_element_type=F32)
    for r in range(SENT2):
        send2[pl.ds(r, devices, stride=8), :] = replies[:, 128 * r:128 * (r + 1)]

    @pl.loop(1, devices)
    def _(n):
        d = lax.rem(me + n, devices)
        pltpu.make_async_remote_copy(
            src_ref=send2.at[pl.ds(pl.multiple_of(d * 8, 8), SENT2)],
            dst_ref=recv2.at[me, pl.ds(0, SENT2)],
            send_sem=s2,
            recv_sem=r2,
            device_id=(d // n_pencil, lax.rem(d, n_pencil)),
            device_id_type=MESH,
        ).start()

    own2 = pltpu.make_async_copy(
        send2.at[pl.ds(my_start, SENT2)], recv2.at[me, pl.ds(0, SENT2)], r2
    )
    own2.start()

    for c in edges2:
        c.wait()
    take_edges(2, pan0)
    outside(image_of)

    @pl.loop(0, 2)
    def _(n):
        for u in range(H // 2):
            vc[n * (H // 2) + u] = vc[n * (H // 2) + u] * inv

    v_copy = pltpu.make_async_copy(vc, out_v, o_sem.at[0])
    v_copy.start()
    pltpu.make_async_copy(
        recv1.at[pl.ds(0, devices * SENT2)], recv1.at[pl.ds(0, devices * SENT2)], r2
    ).wait()

    group8 = lane_group((8, 128))
    low8 = group8 < 2
    sub8 = sublanes((8, 128))

    @pl.loop(0, 2)
    def _(n):
        spots = [(n * (H // 2) + u, g) for u in range(H // 2) for g in range(W // 2)]
        got = [recv2[agg_s[2 * g, i] >> 4] for i, g in spots]
        got = [jnp.where(sub8 < 4, x, pltpu.roll(pltpu.roll(x, 4, 0), 64, 1)) for x in got]
        for (i, g), x in zip(spots, got):
            xg[i, g] = x

    edges3 = []
    for n, (ds, dp) in enumerate(DIRS):
        edge = (H - 1) if ds == 1 else 0
        side = (W // 2 - 1) if dp == 1 else 0
        if dp == 0:
            edges3.append(remote(xg.at[edge], xedge.at[pl.ds(4 * n, 4)], 3, n))
        elif ds == 0:
            edges3.append(
                remote(xg.at[:, side], xedge.at[pl.ds(8 + 16 * (n - 2), H)], 3, n)
            )
        else:
            edges3.append(remote(xg.at[edge, side], xedge.at[40 + n - 4], 3, n))
    for c in edges3:
        c.start()

    even_cell = lax.rem(lanes((32, 128)) // NC, 2) == 0
    xw = pan1

    def fit_weights(fits, places):
        t = fits.T[0:64]
        pieces = jnp.concatenate(split2(t), axis=0).astype(BF16)
        for n in range(8):
            o = jnp.dot(pieces, copier[:, n * 256:(n + 1) * 256], preferred_element_type=F32)
            for u in range(2):
                for cap in range(2):
                    place = places[2 * n + u][cap]
                    if place is None:
                        continue
                    parts = []
                    for p in range(2):
                        x = o[64 * p + 32 * cap:64 * p + 32 * cap + 32, 128 * u:128 * u + 128]
                        parts += [jnp.where(even_cell, x, 0.0), jnp.where(even_cell, 0.0, x)]
                    xw[place] = jnp.concatenate(parts, axis=0).astype(BF16)

    @pl.loop(0, 2)
    def _(n):
        for h in range(2):
            i0 = n * 8 + h * 4
            fits = jnp.concatenate([xg[i0 + u, g] for u in range(4) for g in range(W // 2)], axis=0)
            fit_weights(
                fits,
                [
                    [(i0 + u + 1) * PW + 2 * g + cap + 1 for cap in range(2)]
                    for u in range(4)
                    for g in range(W // 2)
                ],
            )

    lane_q = lanes((8, 128)) // 16
    even_s = lax.rem(sub8, 2) == 0
    two_s = lax.rem(sub8 // 2, 2) == 0
    keep1 = lax.rem(lane_q, 2) == lax.rem(sub8, 2)
    at1 = jnp.where(keep1, lane_q, lax.rem(lane_q + 1, 8))
    keep2 = lax.rem(at1 // 2, 2) == lax.rem(sub8 // 2, 2)
    at2 = jnp.where(keep2, at1, lax.rem(at1 + 2, 8))
    keep3 = at2 == sub8

    def own_rows(s):
        z = [s[8 * r:8 * r + 8] for r in range(4)]

        def merge(x, y, first, keep, shift):
            return jnp.where(
                keep, jnp.where(first, x, y), pltpu.roll(jnp.where(first, y, x), shift, 0)
            )

        u = merge(
            merge(z[0], z[1], even_s, keep1, 1), merge(z[2], z[3], even_s, keep1, 1), two_s, keep2, 2
        )
        return jnp.where(keep3, u, pltpu.roll(u, 4, 0))[0:4]

    def finish(cells):
        for i, j in cells:
            b = i * W + j
            spots = slot_spots(i, j) + [(i + 1) * PW + j + 1]
            for k in range(KS + 1):
                w = wbuf[b * (KS + 1) + k]
                x = [xw[spots[k], 32 * m:32 * m + 32] for m in range(4)]
                s = jnp.dot(
                    jnp.concatenate([w, w], axis=1),
                    jnp.concatenate([x[m // 2] for m in range(8)], axis=0),
                    preferred_element_type=F32,
                )
                if k < KS:
                    prods[i, pl.ds(k * 32 + j, 4, stride=8), :] = own_rows(s)
                else:
                    tiles[i, pl.ds(j, 4, stride=8), :] = own_rows(s)

    inside(finish)
    for c in edges3:
        c.wait()
    places = [[None, None] for _ in range(44)]
    for n, (ds, dp) in enumerate(DIRS):
        row = (0 if ds == 1 else H + 1) * PW
        col = 0 if dp == 1 else W + 1
        cap = 1 if dp == 1 else 0
        if dp == 0:
            for j in range(W):
                places[4 * n + j // 2][j % 2] = row + j + 1
        elif ds == 0:
            for i in range(H):
                places[8 + 16 * (n - 2) + i][cap] = (i + 1) * PW + col
        else:
            places[40 + n - 4][cap] = row + col
    for n in range(3):
        tiles16 = [xedge[16 * n + u] for u in range(16 if n < 2 else 12)]
        tiles16 += [jnp.zeros((8, 128), F32)] * (16 - len(tiles16))
        fit_weights(
            jnp.concatenate(tiles16, axis=0), (places + [[None, None]] * 4)[16 * n:16 * n + 16]
        )
    @pl.loop(0, 2)
    def _(n):
        finish([(1 + 7 * n + u, j) for u in range(7) for j in (0, W - 1)])

    middle = pl.ds(1, H - 2)
    t_mid = pltpu.make_async_copy(tiles.at[middle], out_t.at[middle], o_sem.at[1])
    p_mid = pltpu.make_async_copy(prods.at[middle], out_p.at[middle], o_sem.at[2])
    t_mid.start()
    p_mid.start()
    finish([(i, j) for i in (0, H - 1) for j in range(W)])
    last = []
    for n, i in enumerate((0, H - 1)):
        last.append(pltpu.make_async_copy(tiles.at[i], out_t.at[i], o_sem.at[3 + n]))
        last.append(pltpu.make_async_copy(prods.at[i], out_p.at[i], o_sem.at[5 + n]))
    for c in last:
        c.start()

    def sent(rows, sem):
        part = recv1.at[pl.ds(0, (devices - 1) * rows)]
        pltpu.make_async_copy(part, part, sem).wait()

    sent(SENT1, s1)
    sent(SENT2, s2)
    for c in [v_copy, t_mid, p_mid] + last:
        c.wait()


def mode_blocks():
    centre = np.arange(BLK, dtype=np.float64) + 0.5
    table = np.cos(math.pi * centre[:, None] * np.arange(NC)[None, :] / BLK).astype(np.float32)
    dense = np.einsum("qsm,vw->qsvmw", table.reshape(16, 4, NC), np.eye(NV, dtype=np.float32))
    dense = dense.reshape(16, 4 * NV, NC * NV)
    hi = dense.astype(ml_dtypes.bfloat16)
    lo = (dense - hi.astype(np.float32)).astype(ml_dtypes.bfloat16)
    return np.concatenate([hi, lo], axis=1)


def solution(mesh):
    n_slab = mesh.shape["slab"]
    n_pencil = mesh.shape["pencil"]
    devices = n_slab * n_pencil

    def shards(a_blocks, col_codes, agg_of, test_vectors):
        a = a_blocks.reshape(H, W, 160, 128).transpose(0, 2, 1, 3).reshape(H, 1280, 128)
        tv = test_vectors.reshape(H, W, 16, 128).transpose(0, 2, 1, 3).reshape(H, 128, 128)
        vmem = pl.BlockSpec(memory_space=pltpu.VMEM)
        smem = pl.BlockSpec(memory_space=pltpu.SMEM)
        hbm = pl.BlockSpec(memory_space=pl.ANY)
        dma = pltpu.SemaphoreType.DMA
        out_v, out_t, out_p = pl.pallas_call(
            lambda *refs: body(n_slab, n_pencil, *refs),
            out_shape=(
                jax.ShapeDtypeStruct((H, 128, 128), F32),
                jax.ShapeDtypeStruct((H, 32, 128), F32),
                jax.ShapeDtypeStruct((H, 160, 128), F32),
            ),
            in_specs=[hbm, smem, smem, hbm, hbm],
            out_specs=(hbm, hbm, hbm),
            scratch_shapes=[
                pltpu.VMEM((NB, 1280, 128), F32),
                pltpu.VMEM((H * W * KS, 64, 128), BF16),
                pltpu.VMEM((H * W, 32, 128), F32),
                pltpu.VMEM((H * W, 64, 128), F32),
                pltpu.VMEM((SPOTS, 128, 128), BF16),
                pltpu.VMEM((SPOTS, 128, 128), BF16),
                pltpu.VMEM((H * W * (KS + 1), 32, 128), BF16),
                pltpu.VMEM((16, 256, 256), BF16),
                pltpu.VMEM((128, 2048), BF16),
                pltpu.VMEM((H, 128, 128), F32),
                pltpu.VMEM((H, 128, 128), F32),
                pltpu.VMEM((16, 64, 128), F32),
                pltpu.VMEM((3, 2, 256, 128), F32),
                pltpu.VMEM((3, 2, 128, 128), F32),
                pltpu.VMEM((3, 2, 256, 128), F32),
                pltpu.VMEM((3, 4, 16, 128), F32),
                pltpu.VMEM((16, 16, 128), F32),
                pltpu.VMEM((devices * 8, 128), F32),
                pltpu.VMEM((devices * 8, 128), F32),
                pltpu.VMEM((devices * 8, 128), F32),
                pltpu.VMEM((devices, 8, 128), F32),
                pltpu.VMEM((H, W // 2, 8, 128), F32),
                pltpu.VMEM((44, 8, 128), F32),
                pltpu.VMEM((H, 32, 128), F32),
                pltpu.VMEM((H, 160, 128), F32),
                dma((NB,)),
                dma,
                dma,
                dma((7,)),
                dma((4, 8)),
                dma((4, 8)),
                dma,
                dma,
                dma,
                dma,
            ],
            compiler_params=pltpu.CompilerParams(
                collective_id=0, has_side_effects=True, vmem_limit_bytes=60 * 1024 * 1024
            ),
        )(a, col_codes.transpose(2, 1, 0), agg_of.T, tv, jnp.asarray(mode_blocks()))
        relaxed = out_v.reshape(H, 16, W, 128).transpose(0, 2, 1, 3).reshape(H, W, BLK * NV)
        tiles = out_t.reshape(H, 4, W, 128).transpose(0, 2, 1, 3).reshape(H, W, BLK * NC)
        products = out_p.reshape(H, 20, W, 128).transpose(0, 2, 1, 3).reshape(H, W, KS * BLK * NC)
        return relaxed, tiles, products

    spec = P("slab", "pencil", None)
    return jax.shard_map(
        shards,
        mesh=mesh,
        in_specs=(spec, spec, P("slab", "pencil"), spec),
        out_specs=(spec, spec, spec),
        check_vma=False,
    )
```

```python
import math

import ml_dtypes
import numpy as np
import jax
import jax.numpy as jnp
from jax import lax
from jax.experimental import pallas as pl
from jax.experimental.pallas import tpu as pltpu
from jax.sharding import PartitionSpec as P

BLK = 64
NV = 32
NC = 8
KS = 5
OMEGA = 2.0 / 3.0
MESH = pl.DeviceIdType.MESH
F32 = jnp.float32
BF16 = jnp.bfloat16

H = 16
W = 8
PW = W + 2
SPOTS = (H + 2) * PW
NB = 8
SENT1 = 5
SENT2 = 4

DIRS = [(1, 0), (-1, 0), (0, 1), (0, -1), (1, 1), (1, -1), (-1, 1), (-1, -1)]


def lanes(shape):
    return lax.broadcasted_iota(jnp.int32, shape, len(shape) - 1)


def sublanes(shape):
    return lax.broadcasted_iota(jnp.int32, shape, 0)


def lane_group(shape):
    return lanes(shape) // NV


def split2(x):
    hi = x.astype(BF16).astype(F32)
    return hi, x - hi


def split3(x):
    one = x.astype(BF16)
    rest = x - one.astype(F32)
    two = rest.astype(BF16)
    three = (rest - two.astype(F32)).astype(BF16)
    return one, two, three


def by_group(parts, group):
    out = parts[3]
    for n in (2, 1, 0):
        out = jnp.where(group == n, parts[n], out)
    return out


def body(n_slab, n_pencil, a_hbm, codes, agg_s, tv_hbm, modes_hbm, out_v, out_t, out_p,
         abuf, aprep, dinv, vf, pan0, pan1, wbuf, modes, copier, tv, vc, tmp, colsend, hrow, hcol, hcor,
         sq, send1, recv1, send2, recv2, xg, xedge, tiles, prods,
         a_sem, tv_sem, m_sem, o_sem, hs_sem, hr_sem, s1, r1, s2, r2):
    devices = n_slab * n_pencil
    slab = lax.axis_index("slab")
    pencil = lax.axis_index("pencil")
    me = slab * n_pencil + pencil

    def a_copy(i):
        return pltpu.make_async_copy(
            a_hbm.at[i], abuf.at[lax.rem(i, NB)], a_sem.at[lax.rem(i, NB)]
        )

    tv_copy = pltpu.make_async_copy(tv_hbm, tv, tv_sem)
    tv_copy.start()
    for i in range(NB):
        a_copy(i).start()

    m_copy = pltpu.make_async_copy(modes_hbm, modes, m_sem)
    m_copy.start()
    barrier = pltpu.get_barrier_semaphore()

    @pl.loop(1, devices)
    def _(n):
        d = lax.rem(me + n, devices)
        pl.semaphore_signal(
            barrier, inc=1, device_id=(d // n_pencil, lax.rem(d, n_pencil)), device_id_type=MESH
        )

    group16 = lane_group((16, 128))
    group64 = lane_group((64, 128))
    odd64 = lax.rem(group64, 2) == 1
    low64 = group64 < 2
    group32 = lane_group((32, 128))
    odd32 = lax.rem(group32, 2) == 1
    low32 = group32 < 2

    def spread(x, dst, *lead):
        turns = [x] + [pltpu.roll(x, NV * n, 1) for n in (1, 2, 3)]
        for s in range(4):
            dst[(*lead, pl.ds(s, 16, stride=4), slice(None))] = by_group(
                [turns[(g - s) % 4] for g in range(4)], group16
            )

    def panel_of(v):
        hi, lo = split2(v)
        w = jnp.where(odd64, lo, hi)
        both = jnp.concatenate([jnp.where(low64, w, 0.0), jnp.where(low64, 0.0, w)], axis=0)
        return both.astype(BF16)

    def gather_cells(b):
        return by_group([vf[b, pl.ds(s, 16, stride=4), :] for s in range(4)], group16)

    def remote(src, dst, rnd, n):
        ds, dp = DIRS[n]
        return pltpu.make_async_remote_copy(
            src_ref=src,
            dst_ref=dst,
            send_sem=hs_sem.at[rnd, n],
            recv_sem=hr_sem.at[rnd, n],
            device_id=(lax.rem(slab + ds + n_slab, n_slab), lax.rem(pencil + dp + n_pencil, n_pencil)),
            device_id_type=MESH,
        )

    def edge_copies(rnd, rows):
        copies = []
        for n, (ds, dp) in enumerate(DIRS):
            edge = (H - 1) if ds == 1 else 0
            if dp == 0:
                src, dst = rows.at[edge], hrow.at[rnd, n]
            elif ds == 0:
                src, dst = colsend.at[rnd, n - 2], hcol.at[rnd, n - 2]
            else:
                src = colsend.at[rnd, 0 if dp == 1 else 1, pl.ds(edge * 16, 16)]
                dst = hcor.at[rnd, n - 4]
            copies.append(remote(src, dst, rnd, n))
        return copies

    def from_inside(n):
        ds, dp = DIRS[n]
        ok_s = slab - ds
        ok_p = pencil - dp
        return jnp.logical_and(
            jnp.logical_and(ok_s >= 0, ok_s < n_slab), jnp.logical_and(ok_p >= 0, ok_p < n_pencil)
        )

    def take_edges(rnd, pan):
        for n, (ds, dp) in enumerate(DIRS):
            keep = from_inside(n).astype(F32)
            if dp == 0:
                base = 0 if ds == 1 else (H + 1) * PW
                for j in range(W):
                    spread(hrow[rnd, n, pl.ds(j, 16, stride=8), :] * keep, tmp, n * W + j)
                for j in range(W):
                    pan[base + j + 1] = panel_of(tmp[n * W + j])
            elif ds == 0:
                col = 0 if dp == 1 else W + 1

                for i in range(H):
                    spread(hcol[rnd, n - 2, i * 16:(i + 1) * 16, :] * keep, tmp, i)
                for i in range(H):
                    pan[(i + 1) * PW + col] = panel_of(tmp[i])
            else:
                spot = (0 if ds == 1 else H + 1) * PW + (0 if dp == 1 else W + 1)
                spread(hcor[rnd, n - 4] * keep, tmp, n)
                pan[spot] = panel_of(tmp[n])

    tv_copy.wait()
    for i in range(H):
        colsend[0, 0, i * 16:(i + 1) * 16, :] = tv[i, pl.ds(W - 1, 16, stride=8), :]
        colsend[0, 1, i * 16:(i + 1) * 16, :] = tv[i, pl.ds(0, 16, stride=8), :]

    @pl.loop(0, H // 2)
    def _(n):
        cells = [(2 * n + u, j) for u in range(2) for j in range(W)]
        for i, j in cells:
            spread(tv[i, pl.ds(j, 16, stride=8), :], vf, i * W + j)
        for i, j in cells:
            pan0[(i + 1) * PW + j + 1] = panel_of(vf[i * W + j])

    lane32 = lanes((32, 128))
    row32 = sublanes((32, 128))
    left = lane32 < 64
    on_even = lane32 == 2 * row32
    on_odd = lane32 == 2 * row32 + 65

    @pl.loop(0, H)
    def _(i):
        a_copy(i).wait()
        slot = lax.rem(i, NB)
        for j in range(W):
            b = i * W + j
            for k in range(KS):
                x = abuf[slot, pl.ds(k * 256 + j, 32, stride=8), :]
                hi = x.astype(BF16)
                lo = (x - hi.astype(F32)).astype(BF16)
                aprep[b * KS + k] = jnp.concatenate([hi, lo], axis=0)
                if k == 0:
                    d_even = jnp.sum(jnp.where(on_even, x, 0.0), axis=1, keepdims=True)
                    d_odd = jnp.sum(jnp.where(on_odd, x, 0.0), axis=1, keepdims=True)
                    dinv[b] = OMEGA / jnp.where(left, d_even, d_odd)

        @pl.when(i + NB < H)
        def _():
            a_copy(i + NB).start()

    lane_r = lanes((128, 128))
    row_r = sublanes((128, 128))
    for n in range(16):
        hit = row_r == n * NC + lax.rem(lane_r, NC)
        copier[:, n * 128:(n + 1) * 128] = jnp.where(hit, 1.0, 0.0).astype(BF16)

    def slot_spots(i, j):
        spots = []
        for k in range(KS):
            code = codes[k, j, i]
            di = (code * 11) >> 5
            spots.append((i + di) * PW + j + code - 3 * di)
        return spots

    def relax(cells, old, new, rnd, kept):
        images = []
        for i, j in cells:
            b = i * W + j
            left_side = jnp.concatenate([aprep[b * KS + k] for k in range(KS)], axis=1)
            right = jnp.concatenate([old[spot] for spot in slot_spots(i, j)], axis=0)
            images.append(jnp.dot(left_side, right, preferred_element_type=F32))
        for n, (i, j) in enumerate(cells):
            r = (images[n][0:32] + images[n][32:64]) * dinv[i * W + j]
            r1, r2, r3 = (pltpu.roll(r, NV * m, 1) for m in (1, 2, 3))
            sums = [r + r3, r + r1, r1 + r2, r2 + r3]
            tmp[n, pl.ds(0, 32, stride=2), :] = by_group(sums, group32)
            tmp[n, pl.ds(1, 32, stride=2), :] = by_group(sums[2:] + sums[:2], group32)
        fresh = [vf[i * W + j] - tmp[n] for n, (i, j) in enumerate(cells)]
        for v, (i, j) in zip(fresh, cells):
            vf[i * W + j] = v
        for v, (i, j) in zip(fresh, cells):
            new[(i + 1) * PW + j + 1] = panel_of(v)
        if kept:
            for n, (i, j) in enumerate(cells):
                keep_cells(i, j, rnd, n)

    def keep_cells(i, j, rnd, n):
        x = gather_cells(i * W + j)
        vc[i, pl.ds(j, 16, stride=8), :] = x
        if j in (0, W - 1):
            colsend[rnd, 0 if j else 1, pl.ds(pl.multiple_of(i * 16, 16), 16), :] = x
        if rnd == 2:
            sq[n] += x * x

    def inside(work, first=1, last=H - 1, rows=2):
        @pl.loop(0, (last - first) // rows)
        def _(n):
            work([(first + rows * n + u, j) for u in range(rows) for j in range(1, W - 1)])

    def outside(work):
        @pl.loop(0, 2)
        def _(n):
            work([(1 + 7 * n + u, j) for u in range(7) for j in (0, W - 1)])

        work([(i, j) for i in (0, H - 1) for j in range(W)])

    def first(cells, kept):
        relax(cells, pan0, pan1, 1, kept)

    inside(lambda cells: first(cells, False), 1, 9, 4)
    pl.semaphore_wait(barrier, devices - 1)
    edges0 = edge_copies(0, tv)
    for c in edges0:
        c.start()
    inside(lambda cells: first(cells, False), 9, 15, 3)
    for c in edges0:
        c.wait()
    take_edges(0, pan0)
    outside(lambda cells: first(cells, True))
    edges1 = edge_copies(1, vc)
    for c in edges1:
        c.start()

    sq[...] = jnp.zeros_like(sq)

    def again(cells):
        relax(cells, pan1, pan0, 2, True)

    inside(again, 1, 9, 4)
    inside(again, 9, 15, 3)
    for c in edges1:
        c.wait()
    take_edges(1, pan1)
    outside(again)
    edges2 = edge_copies(2, vc)
    for c in edges2:
        c.start()

    squares = sq[0]
    for n in range(1, 24):
        squares = squares + sq[n]
    squares = jnp.sum(squares, axis=0, keepdims=True)
    squares = squares + pltpu.roll(squares, 64, 1)
    squares = squares + pltpu.roll(squares, 32, 1)

    lane_d = lanes((devices, 128))
    row_d = sublanes((devices, 128))
    group_d = lane_d // NV
    lane1 = lanes((1, 128))
    rows = []
    for j in range(W):
        row = jnp.zeros((1, 128), jnp.int32)
        for i in range(H):
            row = jnp.where(lane1 == i * W + j, agg_s[j, i], row)
        rows.append(row)
    while len(rows) > 1:
        rows = [x + y for x, y in zip(rows[::2], rows[1::2])]
    agg = rows[0]
    mine = jnp.broadcast_to(agg >> 4, (devices, 128)) == row_d
    local = jnp.broadcast_to((agg & 15) + 1, (devices, 128)).astype(F32)
    parity = lane_d & 1
    m_copy.wait()
    coef = jnp.zeros((H * W, 2 * 128), F32)
    for q in range(16):
        x = jnp.concatenate([vc[i, q * 8:(q + 1) * 8, :] for i in range(H)], axis=0)
        hi, lo = split2(x)
        coef = coef + jnp.dot(
            jnp.concatenate([hi, lo, hi], axis=1).astype(BF16),
            jnp.concatenate([modes[q, 0:128], modes[q]], axis=0),
            preferred_element_type=F32,
        )
    parts = jnp.concatenate(split3(coef), axis=0)
    fifth = jnp.broadcast_to(squares, (devices, 128))
    for cap in range(2):
        chosen = jnp.logical_and(mine, parity == cap).astype(F32)
        chosen_b = chosen.astype(BF16)
        packed = jnp.dot(
            jnp.concatenate([chosen_b] * 3, axis=1), parts, preferred_element_type=F32
        )
        send1[pl.ds(2 * cap, devices, stride=8), :] = packed[:, 0:128]
        send1[pl.ds(2 * cap + 1, devices, stride=8), :] = packed[:, 128:256]
        ident = jnp.sum(chosen * local, axis=1, keepdims=True)
        fifth = jnp.where(group_d == cap + 1, ident, fifth)
    send1[pl.ds(4, devices, stride=8), :] = fifth

    my_start = pl.multiple_of(me * 8, 8)

    @pl.loop(1, devices)
    def _(n):
        d = lax.rem(me + n, devices)
        pltpu.make_async_remote_copy(
            src_ref=send1.at[pl.ds(pl.multiple_of(d * 8, 8), SENT1)],
            dst_ref=recv1.at[pl.ds(my_start, SENT1)],
            send_sem=s1,
            recv_sem=r1,
            device_id=(d // n_pencil, lax.rem(d, n_pencil)),
            device_id_type=MESH,
        ).start()

    own1 = pltpu.make_async_copy(
        send1.at[pl.ds(my_start, SENT1)], recv1.at[pl.ds(my_start, SENT1)], r1
    )
    own1.start()

    def image_of(cells):
        for i, j in cells:
            b = i * W + j
            spots = slot_spots(i, j)
            for k in range(KS + 1):
                if k < KS:
                    o = jnp.dot(aprep[b * KS + k], pan0[spots[k]], preferred_element_type=F32)
                    r = o[0:32] + o[32:64]
                    z = r + jnp.where(odd32, pltpu.roll(r, NV, 1), pltpu.roll(r, 128 - NV, 1))
                else:
                    z = jnp.where(
                        low32, vf[b, pl.ds(0, 32, stride=2), :], vf[b, pl.ds(1, 32, stride=2), :]
                    )
                hi, lo = split2(z)
                wbuf[b * (KS + 1) + k] = jnp.where(odd32, lo, hi).astype(BF16)

    inside(image_of)

    pltpu.make_async_copy(
        send1.at[pl.ds(0, devices * SENT1)], recv1.at[pl.ds(0, devices * SENT1)], r1
    ).wait()

    heard = recv1[pl.ds(4, devices, stride=8), :]
    total = jnp.sum(heard, axis=0, keepdims=True)
    total = jnp.where(lane1 < NV, total, 0.0)
    total = total + pltpu.roll(total, 64, 1)
    total = total + pltpu.roll(total, 32, 1)
    inv = 1.0 / jnp.sqrt(total / (H * W * BLK * devices) + 1e-06)

    want = (lane_d + 1).astype(F32)
    few = lane_d < 16
    member_t = [
        jnp.where(jnp.logical_and(pltpu.roll(heard, 128 - NV * (cap + 1), 1) == want, few), 1.0, 0.0)
        for cap in range(2)
    ]
    member = [m.T[0:16] for m in member_t]
    counts = jnp.sum(member[0] + member[1], axis=1, keepdims=True)
    lhs, rhs = [], []
    for cap in range(2):
        rows = jnp.concatenate(
            [recv1[pl.ds(2 * cap + h, devices, stride=8), :] for h in range(2)], axis=1
        )
        lhs += [member[cap].astype(BF16)] * 3
        rhs += list(split3(rows))
    coarse = jnp.dot(
        jnp.concatenate(lhs, axis=1), jnp.concatenate(rhs, axis=0), preferred_element_type=F32
    )
    coarse = coarse * jnp.concatenate([inv, inv], axis=1) / jnp.maximum(counts, 1.0)
    in_first = lanes((16, 128)) < NV
    fit = []
    for k in range(NC):
        half = coarse[:, 128 * (k // 4):128 * (k // 4) + 128]
        if k % 4:
            half = pltpu.roll(half, 128 - NV * (k % 4), 1)
        fit.append(jnp.where(in_first, half, 0.0))
    gram = {}
    for k in range(NC):
        for l in range(k + 1):
            gram[k, l] = jnp.sum(fit[k] * fit[l], axis=1, keepdims=True)
    trace_sum = gram[0, 0]
    for k in range(1, NC):
        trace_sum = trace_sum + gram[k, k]
    ridge = 0.1 * trace_sum / NC + 1e-06
    low, raw, pivot = {}, {}, {}
    for k in range(NC):
        top = gram[k, k] + ridge
        for l in range(k):
            top = top - raw[k, l] * low[k, l]
        pivot[k] = 1.0 / top
        for m in range(k + 1, NC):
            val = gram[m, k]
            for l in range(k):
                val = val - raw[m, l] * low[k, l]
            raw[m, k] = val
            low[m, k] = val * pivot[k]
    sol = []
    for k in range(NC):
        y = fit[k]
        for l in range(k):
            y = y - low[k, l] * sol[l]
        sol.append(y)
    for k in range(NC):
        sol[k] = sol[k] * pivot[k]
    for k in reversed(range(NC)):
        for l in range(k + 1, NC):
            sol[k] = sol[k] - low[l, k] * sol[l]
    columns = []
    for r in range(SENT2):
        pair = sol[r] * inv + pltpu.roll(sol[r + 4] * inv, 64, 1)
        columns.append(jnp.concatenate([pair, pltpu.roll(pair, NV, 1)], axis=0))
    pieces = list(split3(jnp.concatenate(columns, axis=1)))
    table = jnp.concatenate(pieces + [jnp.zeros_like(pieces[0])], axis=0)
    pick = member_t[0] + pltpu.roll(member_t[1], 16, 1)
    pick = pick + pltpu.roll(pick, 32, 1) + pltpu.roll(pick, 64, 1)
    replies = jnp.dot(pick.astype(BF16), table, preferred_element_type=F32)
    for r in range(SENT2):
        send2[pl.ds(r, devices, stride=8), :] = replies[:, 128 * r:128 * (r + 1)]

    @pl.loop(1, devices)
    def _(n):
        d = lax.rem(me + n, devices)
        pltpu.make_async_remote_copy(
            src_ref=send2.at[pl.ds(pl.multiple_of(d * 8, 8), SENT2)],
            dst_ref=recv2.at[me, pl.ds(0, SENT2)],
            send_sem=s2,
            recv_sem=r2,
            device_id=(d // n_pencil, lax.rem(d, n_pencil)),
            device_id_type=MESH,
        ).start()

    own2 = pltpu.make_async_copy(
        send2.at[pl.ds(my_start, SENT2)], recv2.at[me, pl.ds(0, SENT2)], r2
    )
    own2.start()

    for c in edges2:
        c.wait()
    take_edges(2, pan0)
    outside(image_of)

    @pl.loop(0, 2)
    def _(n):
        for u in range(H // 2):
            vc[n * (H // 2) + u] = vc[n * (H // 2) + u] * inv

    v_copy = pltpu.make_async_copy(vc, out_v, o_sem.at[0])
    v_copy.start()
    pltpu.make_async_copy(
        recv1.at[pl.ds(0, devices * SENT2)], recv1.at[pl.ds(0, devices * SENT2)], r2
    ).wait()

    group8 = lane_group((8, 128))
    low8 = group8 < 2
    sub8 = sublanes((8, 128))

    @pl.loop(0, 2)
    def _(n):
        spots = [(n * (H // 2) + u, g) for u in range(H // 2) for g in range(W // 2)]
        got = [recv2[agg_s[2 * g, i] >> 4] for i, g in spots]
        got = [jnp.where(sub8 < 4, x, pltpu.roll(pltpu.roll(x, 4, 0), 64, 1)) for x in got]
        for (i, g), x in zip(spots, got):
            xg[i, g] = x

    edges3 = []
    for n, (ds, dp) in enumerate(DIRS):
        edge = (H - 1) if ds == 1 else 0
        side = (W // 2 - 1) if dp == 1 else 0
        if dp == 0:
            edges3.append(remote(xg.at[edge], xedge.at[pl.ds(4 * n, 4)], 3, n))
        elif ds == 0:
            edges3.append(
                remote(xg.at[:, side], xedge.at[pl.ds(8 + 16 * (n - 2), H)], 3, n)
            )
        else:
            edges3.append(remote(xg.at[edge, side], xedge.at[40 + n - 4], 3, n))
    for c in edges3:
        c.start()

    even_cell = lax.rem(lanes((32, 128)) // NC, 2) == 0
    xw = pan1

    def fit_weights(fits, places):
        t = fits.T[0:64]
        pieces = jnp.concatenate(split2(t), axis=0).astype(BF16)
        for n in range(8):
            o = jnp.dot(pieces, copier[:, n * 256:(n + 1) * 256], preferred_element_type=F32)
            for u in range(2):
                for cap in range(2):
                    place = places[2 * n + u][cap]
                    if place is None:
                        continue
                    parts = []
                    for p in range(2):
                        x = o[64 * p + 32 * cap:64 * p + 32 * cap + 32, 128 * u:128 * u + 128]
                        parts += [jnp.where(even_cell, x, 0.0), jnp.where(even_cell, 0.0, x)]
                    xw[place] = jnp.concatenate(parts, axis=0).astype(BF16)

    @pl.loop(0, 2)
    def _(n):
        for h in range(2):
            i0 = n * 8 + h * 4
            fits = jnp.concatenate([xg[i0 + u, g] for u in range(4) for g in range(W // 2)], axis=0)
            fit_weights(
                fits,
                [
                    [(i0 + u + 1) * PW + 2 * g + cap + 1 for cap in range(2)]
                    for u in range(4)
                    for g in range(W // 2)
                ],
            )

    lane_q = lanes((8, 128)) // 16
    even_s = lax.rem(sub8, 2) == 0
    two_s = lax.rem(sub8 // 2, 2) == 0
    keep1 = lax.rem(lane_q, 2) == lax.rem(sub8, 2)
    at1 = jnp.where(keep1, lane_q, lax.rem(lane_q + 1, 8))
    keep2 = lax.rem(at1 // 2, 2) == lax.rem(sub8 // 2, 2)
    at2 = jnp.where(keep2, at1, lax.rem(at1 + 2, 8))
    keep3 = at2 == sub8

    def own_rows(s):
        z = [s[8 * r:8 * r + 8] for r in range(4)]

        def merge(x, y, first, keep, shift):
            return jnp.where(
                keep, jnp.where(first, x, y), pltpu.roll(jnp.where(first, y, x), shift, 0)
            )

        u = merge(
            merge(z[0], z[1], even_s, keep1, 1), merge(z[2], z[3], even_s, keep1, 1), two_s, keep2, 2
        )
        return jnp.where(keep3, u, pltpu.roll(u, 4, 0))[0:4]

    def finish(cells):
        for i, j in cells:
            b = i * W + j
            spots = slot_spots(i, j) + [(i + 1) * PW + j + 1]
            for k in range(KS + 1):
                w = wbuf[b * (KS + 1) + k]
                x = [xw[spots[k], 32 * m:32 * m + 32] for m in range(4)]
                s = jnp.dot(
                    jnp.concatenate([w, w], axis=1),
                    jnp.concatenate([x[m // 2] for m in range(8)], axis=0),
                    preferred_element_type=F32,
                )
                if k < KS:
                    prods[i, pl.ds(k * 32 + j, 4, stride=8), :] = own_rows(s)
                else:
                    tiles[i, pl.ds(j, 4, stride=8), :] = own_rows(s)

    inside(finish)
    for c in edges3:
        c.wait()
    places = [[None, None] for _ in range(44)]
    for n, (ds, dp) in enumerate(DIRS):
        row = (0 if ds == 1 else H + 1) * PW
        col = 0 if dp == 1 else W + 1
        cap = 1 if dp == 1 else 0
        if dp == 0:
            for j in range(W):
                places[4 * n + j // 2][j % 2] = row + j + 1
        elif ds == 0:
            for i in range(H):
                places[8 + 16 * (n - 2) + i][cap] = (i + 1) * PW + col
        else:
            places[40 + n - 4][cap] = row + col
    for n in range(3):
        tiles16 = [xedge[16 * n + u] for u in range(16 if n < 2 else 12)]
        tiles16 += [jnp.zeros((8, 128), F32)] * (16 - len(tiles16))
        fit_weights(
            jnp.concatenate(tiles16, axis=0), (places + [[None, None]] * 4)[16 * n:16 * n + 16]
        )
    @pl.loop(0, 2)
    def _(n):
        finish([(1 + 7 * n + u, j) for u in range(7) for j in (0, W - 1)])

    middle = pl.ds(1, H - 2)
    t_mid = pltpu.make_async_copy(tiles.at[middle], out_t.at[middle], o_sem.at[1])
    p_mid = pltpu.make_async_copy(prods.at[middle], out_p.at[middle], o_sem.at[2])
    t_mid.start()
    p_mid.start()
    finish([(i, j) for i in (0, H - 1) for j in range(W)])
    last = []
    for n, i in enumerate((0, H - 1)):
        last.append(pltpu.make_async_copy(tiles.at[i], out_t.at[i], o_sem.at[3 + n]))
        last.append(pltpu.make_async_copy(prods.at[i], out_p.at[i], o_sem.at[5 + n]))
    for c in last:
        c.start()

    def sent(rows, sem):
        part = recv1.at[pl.ds(0, (devices - 1) * rows)]
        pltpu.make_async_copy(part, part, sem).wait()

    sent(SENT1, s1)
    sent(SENT2, s2)
    for c in [v_copy, t_mid, p_mid] + last:
        c.wait()


def mode_blocks():
    centre = np.arange(BLK, dtype=np.float64) + 0.5
    table = np.cos(math.pi * centre[:, None] * np.arange(NC)[None, :] / BLK).astype(np.float32)
    dense = np.einsum("qsm,vw->qsvmw", table.reshape(16, 4, NC), np.eye(NV, dtype=np.float32))
    dense = dense.reshape(16, 4 * NV, NC * NV)
    hi = dense.astype(ml_dtypes.bfloat16)
    lo = (dense - hi.astype(np.float32)).astype(ml_dtypes.bfloat16)
    return np.concatenate([hi, lo], axis=1)


def solution(mesh):
    n_slab = mesh.shape["slab"]
    n_pencil = mesh.shape["pencil"]
    devices = n_slab * n_pencil

    def shards(a_blocks, col_codes, agg_of, test_vectors):
        a = a_blocks.reshape(H, W, 160, 128).transpose(0, 2, 1, 3).reshape(H, 1280, 128)
        tv = test_vectors.reshape(H, W, 16, 128).transpose(0, 2, 1, 3).reshape(H, 128, 128)
        vmem = pl.BlockSpec(memory_space=pltpu.VMEM)
        smem = pl.BlockSpec(memory_space=pltpu.SMEM)
        hbm = pl.BlockSpec(memory_space=pl.ANY)
        dma = pltpu.SemaphoreType.DMA
        out_v, out_t, out_p = pl.pallas_call(
            lambda *refs: body(n_slab, n_pencil, *refs),
            out_shape=(
                jax.ShapeDtypeStruct((H, 128, 128), F32),
                jax.ShapeDtypeStruct((H, 32, 128), F32),
                jax.ShapeDtypeStruct((H, 160, 128), F32),
            ),
            in_specs=[hbm, smem, smem, hbm, hbm],
            out_specs=(hbm, hbm, hbm),
            scratch_shapes=[
                pltpu.VMEM((NB, 1280, 128), F32),
                pltpu.VMEM((H * W * KS, 64, 128), BF16),
                pltpu.VMEM((H * W, 32, 128), F32),
                pltpu.VMEM((H * W, 64, 128), F32),
                pltpu.VMEM((SPOTS, 128, 128), BF16),
                pltpu.VMEM((SPOTS, 128, 128), BF16),
                pltpu.VMEM((H * W * (KS + 1), 32, 128), BF16),
                pltpu.VMEM((16, 256, 256), BF16),
                pltpu.VMEM((128, 2048), BF16),
                pltpu.VMEM((H, 128, 128), F32),
                pltpu.VMEM((H, 128, 128), F32),
                pltpu.VMEM((24, 64, 128), F32),
                pltpu.VMEM((3, 2, 256, 128), F32),
                pltpu.VMEM((3, 2, 128, 128), F32),
                pltpu.VMEM((3, 2, 256, 128), F32),
                pltpu.VMEM((3, 4, 16, 128), F32),
                pltpu.VMEM((24, 16, 128), F32),
                pltpu.VMEM((devices * 8, 128), F32),
                pltpu.VMEM((devices * 8, 128), F32),
                pltpu.VMEM((devices * 8, 128), F32),
                pltpu.VMEM((devices, 8, 128), F32),
                pltpu.VMEM((H, W // 2, 8, 128), F32),
                pltpu.VMEM((44, 8, 128), F32),
                pltpu.VMEM((H, 32, 128), F32),
                pltpu.VMEM((H, 160, 128), F32),
                dma((NB,)),
                dma,
                dma,
                dma((7,)),
                dma((4, 8)),
                dma((4, 8)),
                dma,
                dma,
                dma,
                dma,
            ],
            compiler_params=pltpu.CompilerParams(
                collective_id=0, has_side_effects=True, vmem_limit_bytes=60 * 1024 * 1024
            ),
        )(a, col_codes.transpose(2, 1, 0), agg_of.T, tv, jnp.asarray(mode_blocks()))
        relaxed = out_v.reshape(H, 16, W, 128).transpose(0, 2, 1, 3).reshape(H, W, BLK * NV)
        tiles = out_t.reshape(H, 4, W, 128).transpose(0, 2, 1, 3).reshape(H, W, BLK * NC)
        products = out_p.reshape(H, 20, W, 128).transpose(0, 2, 1, 3).reshape(H, W, KS * BLK * NC)
        return relaxed, tiles, products

    spec = P("slab", "pencil", None)
    return jax.shard_map(
        shards,
        mesh=mesh,
        in_specs=(spec, spec, P("slab", "pencil"), spec),
        out_specs=(spec, spec, spec),
        check_vma=False,
    )
```
